32 devices in a mesh: seq: 4 (over z), fsdp: 8 (over y, x, core).
Axes of the slice: x: 2, y: 2, z: 4, core: 2. Of those that a mesh axis runs over, the one named last changes fastest.
Arguments:
- middle_state: bfloat16 [8, 2048, 4096], P('fsdp', 'seq'), may hold values from -80 to 80
- newest_state: bfloat16 [8, 2048, 4096], P('fsdp', 'seq'), may hold values from -6 to 6
- middle_cotangent: bfloat16 [8, 2048, 4096], P('fsdp', 'seq'), may hold values from -6 to 6
- newest_cotangent: bfloat16 [8, 2048, 4096], P('fsdp', 'seq'), may hold values from -6 to 6
- log_decay: int32 [8, 2048, 32], P('fsdp', 'seq'), may hold values from -3079 to 0
- state_weights: bfloat16 [4096, 256], P('fsdp'), may hold values from -0.09375 to 0.09375
- skip_gain: float32 [32], replicated, may hold values from 0.5 to 1.5
Outputs:
- rebuilt_oldest: bfloat16 [8, 2048, 4096], P('fsdp', 'seq')
- middle_gradient: bfloat16 [8, 2048, 4096], P('fsdp', 'seq')
- weights_gradient: float32 [4096, 256], P(('seq', 'fsdp'))
The draws below stay inside these ranges and needn't reach their ends.
All inputs are finite; a program needn't handle non-finite values.
Results may differ from the reference program's by a relative error of at most 0.017.
Values may be sent and summed in bfloat16 or wider, within the bound.
No kernel may reach another device: no remote copies, remote signals or barrier semaphores. Data moves between devices by JAX's collectives and lax.ppermute only.
A program may use at most 256 MiB of HBM per device.

```python
import jax
import jax.numpy as jnp
from jax import lax

D = 4096
HALF_HEADS = 32
P_SIZE = 128
N = 128
GROUP = 256
TOK_DEV = 512
SEQUENCE_COUNT = 8
SEQUENCE_LENGTH = 2048


def draw_log_decay(key, part):
    random_keys = jax.random.split(jax.random.fold_in(key, 11), 8)
    block_count = SEQUENCE_LENGTH // TOK_DEV
    fast_heads = jax.random.randint(random_keys[0], (SEQUENCE_COUNT, 1, HALF_HEADS), 0, 2)
    base_rate = jax.random.randint(random_keys[1], (SEQUENCE_COUNT, 1, HALF_HEADS), 40, 81)
    block_factor = jax.random.randint(random_keys[2], (SEQUENCE_COUNT, block_count, 1, HALF_HEADS), 2, 5)
    block_factor = jnp.broadcast_to(block_factor, (SEQUENCE_COUNT, block_count, TOK_DEV, HALF_HEADS)).reshape(SEQUENCE_COUNT, SEQUENCE_LENGTH, HALF_HEADS)
    jitter = jax.random.randint(random_keys[3], (SEQUENCE_COUNT, SEQUENCE_LENGTH, HALF_HEADS), 2, 7)
    fast_rate = base_rate * block_factor * jitter // 8
    slow_level = jax.random.randint(random_keys[4], (SEQUENCE_COUNT, block_count, 1, HALF_HEADS), 1, 4)
    slow_level = jnp.broadcast_to(slow_level, (SEQUENCE_COUNT, block_count, TOK_DEV, HALF_HEADS)).reshape(SEQUENCE_COUNT, SEQUENCE_LENGTH, HALF_HEADS)
    slow_pick = jax.random.randint(random_keys[5], (SEQUENCE_COUNT, SEQUENCE_LENGTH, HALF_HEADS), 0, 4)
    slow_rate = jnp.where(slow_pick < slow_level, 1, 0)
    every_rate = jnp.where(fast_heads == 1, fast_rate, slow_rate)
    spike_position = jax.random.randint(random_keys[6], (SEQUENCE_COUNT, 2), 0, SEQUENCE_LENGTH)
    token_positions = jnp.arange(SEQUENCE_LENGTH)
    spike_mask = jnp.any(token_positions[None, :, None] == spike_position[:, None, :], axis=-1)
    spike_scale = jax.random.randint(random_keys[7], (SEQUENCE_COUNT, SEQUENCE_LENGTH, HALF_HEADS), 914, 2840)
    every_rate = every_rate + jnp.where(spike_mask[:, :, None], spike_scale, 0)
    return (-every_rate).astype(jnp.int32)


def draw_middle_state(key, part):
    random_keys = jax.random.split(jax.random.fold_in(key, 23), 3)
    row_scale = jnp.exp(jax.random.uniform(random_keys[0], (SEQUENCE_COUNT, SEQUENCE_LENGTH, 1), jnp.float32, 0.0, 2.31))
    column_scale = jnp.exp(jax.random.uniform(random_keys[1], (1, 1, D), jnp.float32, 0.0, 2.31))
    values = jax.random.normal(random_keys[2], (SEQUENCE_COUNT, SEQUENCE_LENGTH, D), jnp.float32) * row_scale * column_scale * 0.1
    return jnp.clip(values, -80.0, 80.0).astype(jnp.bfloat16)


def block_scale(own_key, shape, cuts, smallest, high):
    gain = 1.0
    for position, blocks in cuts:
        steps = jax.random.uniform(jax.random.fold_in(jax.random.fold_in(own_key, 6), position), (blocks,), jnp.float32, smallest / len(cuts), high / len(cuts))
        gain = gain * jnp.repeat(jnp.exp(steps), shape[position] // blocks).reshape((-1,) + (1,) * (len(shape) - 1 - position))
    return gain


def gaussian(stream_key, extent, scale, most, cuts=(), dtype=jnp.bfloat16):
    factor_of = block_scale(stream_key, extent, cuts, -0.22, 0.18) if cuts else 1.0
    array = jax.random.normal(stream_key, extent, jnp.float32) * scale * factor_of
    return jnp.minimum(jnp.maximum(array, -most), most).astype(dtype)


def setup_inputs(seed: int = 0) -> dict:
    streams_of = jax.random.split(jax.random.key(seed), 8)
    middle_state = draw_middle_state(jax.random.fold_in(streams_of[7], 71), 0)
    newest_state = gaussian(streams_of[1], (SEQUENCE_COUNT, SEQUENCE_LENGTH, D), 1.0, 6.0, ((0, 8), (1, 4)))
    middle_cotangent = gaussian(streams_of[2], (SEQUENCE_COUNT, SEQUENCE_LENGTH, D), 1.0, 6.0, ((0, 8), (1, 4)))
    newest_cotangent = gaussian(streams_of[3], (SEQUENCE_COUNT, SEQUENCE_LENGTH, D), 1.0, 6.0, ((0, 8), (1, 4)))
    log_decay = draw_log_decay(jax.random.fold_in(streams_of[7], 71), 0)
    state_weights = gaussian(streams_of[5], (D, 2 * N), D ** -0.5, 0.09375, ((0, 8),))
    skip_gain = jnp.clip(jax.random.uniform(streams_of[6], (HALF_HEADS,), jnp.float32, 0.5, 1.5), 0.5, 1.5)
    return dict(middle_state=middle_state, newest_state=newest_state, middle_cotangent=middle_cotangent, newest_cotangent=newest_cotangent, log_decay=log_decay, state_weights=state_weights, skip_gain=skip_gain)


highest = lax.Precision.HIGHEST
norm_epsilon = 1e-05
decay_unit = 1.0 / 4096.0

def normalize(values):
    return values * lax.rsqrt(lax.optimization_barrier(jnp.mean(values * values, axis=-1, keepdims=True)) + norm_epsilon)

def group_pass(state_now, pieces, skip_gain):
    features, entry_key, readout, log_rates = pieces
    length = log_rates.shape[0]
    running = jnp.cumsum(log_rates, axis=0)
    input_feed = jnp.sqrt(1.0 - jnp.exp(2.0 * log_rates))
    inputs = features * input_feed[:, :, None]
    scores = jnp.dot(readout, entry_key.T, precision=highest)
    later_index = lax.broadcasted_iota(jnp.int32, (length, length), 0)
    earlier_index = lax.broadcasted_iota(jnp.int32, (length, length), 1)
    causal = (later_index >= earlier_index)[None]
    heads_first = running.T
    log_gaps = heads_first[:, :, None] - heads_first[:, None, :]
    mix_weights = jnp.where(causal, jnp.exp(jnp.where(causal, log_gaps, 0.0)), 0.0) * scores[None]
    within = jnp.einsum('hts,shp->thp', mix_weights, inputs, precision=highest)
    carried = jnp.einsum('tn,hpn->thp', readout, state_now, precision=highest) * jnp.exp(running)[:, :, None]
    outputs = (within + carried) * N ** (-0.5) + skip_gain[None, :, None] * features
    tail_decay = jnp.exp(running[-1][None, :] - running)
    new_state = state_now * jnp.exp(running[-1])[:, None, None] + jnp.einsum('shp,sn->hpn', inputs * tail_decay[:, :, None], entry_key, precision=highest)
    return (new_state, outputs)

def run_rows(feature_values, projected_values, log_rates, skip_gain, start_state):
    row_count = feature_values.shape[0]
    block_count = row_count // GROUP
    features = feature_values.reshape(block_count, GROUP, HALF_HEADS, P_SIZE)
    entry_key = projected_values[:, :N].reshape(block_count, GROUP, N)
    readout = projected_values[:, N:].reshape(block_count, GROUP, N)
    log_blocks = log_rates.reshape(block_count, GROUP, HALF_HEADS)

    def step_block(state_now, pieces):
        return group_pass(state_now, pieces, skip_gain)
    final_state, outputs = lax.scan(step_block, start_state, (features, entry_key, readout, log_blocks))
    return (outputs.reshape(row_count, HALF_HEADS * P_SIZE), final_state)

def reference(middle_state, newest_state, middle_cotangent, newest_cotangent, log_decay, state_weights, skip_gain):
    row_count = middle_state.shape[1]
    zero_start = jnp.zeros((HALF_HEADS, P_SIZE, N), jnp.float32)

    def per_sequence(running_sum, pieces):
        middle, newest, middle_back, newest_back, log_ints = pieces
        normed, norm_back = jax.vjp(normalize, middle.astype(jnp.float32))
        features = normed.astype(jnp.bfloat16)
        projected = jnp.dot(features, state_weights, preferred_element_type=jnp.float32).astype(jnp.bfloat16)
        log_rates = log_ints.astype(jnp.float32) * decay_unit

        def whole_mix(feature_values, projected_values):
            return run_rows(feature_values, projected_values, log_rates, skip_gain, zero_start)[0]
        mixed_out, mix_back = jax.vjp(whole_mix, features.astype(jnp.float32), projected.astype(jnp.float32))
        rebuilt = (newest.astype(jnp.float32) - mixed_out).astype(jnp.bfloat16)
        feature_grad, projected_grad = mix_back(newest_back.astype(jnp.float32))
        projected_low = projected_grad.astype(jnp.bfloat16)
        through_weights = lax.dot_general(projected_low, state_weights, (((1,), (1,)), ((), ())), preferred_element_type=jnp.float32)
        norm_grad, = norm_back(feature_grad + through_weights)
        gradient = (middle_back.astype(jnp.float32) + norm_grad).astype(jnp.bfloat16)
        weight_term = lax.dot_general(features, projected_low, (((0,), (0,)), ((), ())), preferred_element_type=jnp.float32)
        return (running_sum + weight_term, (rebuilt, gradient))
    total_grad, (rebuilt_all, gradient_all) = lax.scan(per_sequence, jnp.zeros((D, 2 * N), jnp.float32), (middle_state, newest_state, middle_cotangent, newest_cotangent, log_decay))
    return (rebuilt_all, gradient_all, total_grad * (SEQUENCE_COUNT * row_count) ** (-0.5))
```

```python
import functools

import jax
import jax.numpy as jnp
from jax import lax
from jax.experimental import pallas as pl
from jax.experimental.pallas import tpu as pltpu
from jax.sharding import PartitionSpec as P

CHUNK = 128
PIECES = 8
SKEW = 2
VMEM_BYTES = 60 * 1024 * 1024

f32 = jnp.float32
bf16 = jnp.bfloat16
norm_epsilon = 1e-05
decay_unit = 1.0 / 4096.0


def dot(a, b, ca, cb):
    return lax.dot_general(a, b, (((ca,), (cb,)), ((), ())), preferred_element_type=f32)


def params():
    return pltpu.CompilerParams(vmem_limit_bytes=VMEM_BYTES)


def cost(flops, nbytes):
    return pl.CostEstimate(flops=int(flops), bytes_accessed=int(nbytes), transcendentals=0)


def shape(s, d):
    return jax.ShapeDtypeStruct(s, d)


def prepare_kernel(mid, cot, decay, x_o, v_o, g_o, rstd_o, a_o, b_o, half_o, *, heads):
    q, d = mid.shape
    ps = d // heads
    values = mid[...].astype(f32)
    rstd = lax.rsqrt(jnp.mean(values * values, axis=-1, keepdims=True) + norm_epsilon)
    rstd_o[...] = rstd
    normed = (values * rstd).astype(bf16)
    x_o[...] = normed
    rates = decay[...].astype(f32)
    later = lax.broadcasted_iota(jnp.int32, (q, q), 0) >= lax.broadcasted_iota(jnp.int32, (q, q), 1)
    running = (
        jnp.dot(later.astype(f32), rates, precision=lax.Precision.HIGHEST, preferred_element_type=f32)
        * decay_unit
    )
    mid_log = 0.5 * running[q - 1 : q, :]
    a = jnp.exp(running - mid_log) * (ps ** (-0.5))
    b = jnp.exp(mid_log - running) * jnp.sqrt(1.0 - jnp.exp(2.0 * (rates * decay_unit)))
    a_o[...] = a
    b_o[...] = b
    half = jnp.exp(mid_log)
    for h in range(heads):
        cols = slice(h * ps, (h + 1) * ps)
        v_o[:, cols] = (x_o[:, cols].astype(f32) * b[:, h : h + 1]).astype(bf16)
        g_o[:, cols] = (cot[:, cols].astype(f32) * a[:, h : h + 1]).astype(bf16)
        half_o[0, :, cols] = jnp.broadcast_to(half[:, h : h + 1], (8, ps))


def prepare(mid, cot, decay):
    t, d = mid.shape
    heads = decay.shape[1]
    n = t // CHUNK
    row = lambda w: pl.BlockSpec((CHUNK, w), lambda i: (i, 0))
    return pl.pallas_call(
        functools.partial(prepare_kernel, heads=heads),
        grid=(n,),
        in_specs=[row(d), row(d), row(heads)],
        out_specs=[row(d), row(d), row(d), row(1), row(heads), row(heads),
                   pl.BlockSpec((1, 8, d), lambda i: (i, 0, 0))],
        out_shape=[shape((t, d), bf16)] * 3
        + [shape((t, 1), f32), shape((t, heads), f32), shape((t, heads), f32), shape((n, 8, d), f32)],
        compiler_params=params(),
        cost_estimate=cost(30 * t * d, 10 * t * d),
        name="prepare",
    )(mid, cot, decay)


def project_kernel(f_ref, x, *refs, keys, block):
    weights, out = refs[:-1], refs[-1]
    f = f_ref[0]
    total = None
    for (k, lo), w in zip(keys, weights):
        start = pl.multiple_of(jnp.bitwise_xor(f, k) * block + lo, 128)
        part = dot(x[:, pl.ds(start, w.shape[0])], w[...], 1, 0)
        total = part if total is None else total + part
    out[...] = total.astype(bf16)


def project(f, x, keys, pieces, block):
    t, d = x.shape
    n2 = pieces[0].shape[1]
    full = pl.BlockSpec(memory_space=pltpu.VMEM)
    return pl.pallas_call(
        functools.partial(project_kernel, keys=keys, block=block),
        in_specs=[pl.BlockSpec(memory_space=pltpu.SMEM), full] + [full] * len(pieces),
        out_specs=full,
        out_shape=shape((t, n2), bf16),
        compiler_params=params(),
        cost_estimate=cost(2 * t * d * n2, 2 * (t * d + d * n2)),
        name="project",
    )(f, x, *pieces)


def states_kernel(p, v, g, half, sl_o, dl_o, sloc_o, dloc_o, dtot_o):
    t, w = v.shape
    n = p.shape[1] // 2
    count = t // CHUNK
    state = jnp.zeros((n, w), f32)
    total = jnp.ones((8, w), f32)
    for k in range(count):
        rows = slice(k * CHUNK, (k + 1) * CHUNK)
        hk = half[k, 0:1, :]
        state = state * hk
        sl_o[k] = state.astype(bf16)
        state = (state + dot(p[rows, :n], v[rows, :], 0, 0)) * hk
        total = total * half[k] * half[k]
    sloc_o[0] = state.astype(bf16)
    dtot_o[...] = total
    state = jnp.zeros((n, w), f32)
    for k in reversed(range(count)):
        rows = slice(k * CHUNK, (k + 1) * CHUNK)
        hk = half[k, 0:1, :]
        state = state * hk
        dl_o[k] = state.astype(bf16)
        state = (state + dot(p[rows, n:], g[rows, :], 0, 0)) * hk
    dloc_o[0] = state.astype(bf16)


def states(p, v, g, half):
    t, d = v.shape
    n = p.shape[1] // 2
    count = t // CHUNK
    w = d // PIECES
    cols = pl.BlockSpec((t, w), lambda i: (0, i))
    chunked = pl.BlockSpec((count, n, w), lambda i: (0, 0, i))
    piece = pl.BlockSpec((1, n, w), lambda i: (i, 0, 0))
    return pl.pallas_call(
        states_kernel,
        grid=(PIECES,),
        in_specs=[pl.BlockSpec((t, 2 * n), lambda i: (0, 0)), cols, cols,
                  pl.BlockSpec((count, 8, w), lambda i: (0, 0, i))],
        out_specs=[chunked, chunked, piece, piece, pl.BlockSpec((8, w), lambda i: (0, i))],
        out_shape=[shape((count, n, d), bf16)] * 2 + [shape((PIECES, n, w), bf16)] * 2
        + [shape((8, d), f32)],
        compiler_params=params(),
        cost_estimate=cost(4 * t * d * n, 8 * t * d),
        name="states",
    )(p, v, g, half)


def hop_kernel(ids, rf, rb, lf, lb, df, db, si, di, of, ob, so, do):
    del ids, si, di
    so[...] = rf[...][None]
    do[...] = rb[...][None]
    of[...] = (lf[0].astype(f32) + df[0:1, :] * rf[...].astype(f32)).astype(bf16)
    ob[...] = (lb[0].astype(f32) + db[0:1, :] * rb[...].astype(f32)).astype(bf16)


def hop(ids, j, rf, rb, lf, lb, dtot, si, di):
    n, w = rf.shape
    whole = pl.BlockSpec((n, w), lambda i, s: (0, 0))
    own = lambda c: pl.BlockSpec((1, n, w), lambda i, s: (s[4 * j + c], 0, 0))
    dec = lambda c: pl.BlockSpec((8, w), lambda i, s: (0, s[4 * j + c]))
    anyspace = pl.BlockSpec(memory_space=pl.ANY)
    return pl.pallas_call(
        hop_kernel,
        grid_spec=pltpu.PrefetchScalarGridSpec(
            num_scalar_prefetch=1,
            grid=(1,),
            in_specs=[whole, whole, own(0), own(2), dec(0), dec(2), anyspace, anyspace],
            out_specs=[whole, whole, own(1), own(3)],
        ),
        out_shape=[shape((n, w), bf16)] * 2 + [shape(si.shape, bf16)] * 2,
        input_output_aliases={7: 2, 8: 3},
        compiler_params=params(),
        cost_estimate=cost(4 * n * w, 16 * n * w),
        name="hop",
    )(ids, rf, rb, lf, lb, dtot, dtot, si, di)


def pass_states(sloc, dloc, dtot):
    count = lax.axis_size("seq")
    z = lax.axis_index("seq")
    _, n, w = sloc.shape
    steps = PIECES + SKEW * (count - 1)
    j = jnp.arange(steps, dtype=jnp.int32)

    def indices(place):
        at = j - SKEW * place
        inside = (at >= 0) & (at < PIECES)
        return jnp.clip(at, 0, PIECES - 1), jnp.where(inside, at, PIECES)

    ids = jnp.stack(indices(z) + indices(count - 1 - z), axis=1).reshape(-1)
    onward = [(i, i + 1) for i in range(count - 1)]
    backward = [(i + 1, i) for i in range(count - 1)]
    si = jnp.zeros((PIECES + 1, n, w), bf16)
    di = jnp.zeros((PIECES + 1, n, w), bf16)
    arrived = []
    for step in range(steps):
        if step < SKEW:
            sf = lax.dynamic_index_in_dim(sloc, ids[4 * step], 0, False)
            sb = lax.dynamic_index_in_dim(dloc, ids[4 * step + 2], 0, False)
        else:
            rf, rb = arrived[step - SKEW]
            sf, sb, si, di = hop(ids, step, rf, rb, sloc, dloc, dtot, si, di)
        if step < steps - SKEW:
            arrived.append((lax.ppermute(sf, "seq", onward), lax.ppermute(sb, "seq", backward)))
    return si, di


def causal(q):
    return lax.broadcasted_iota(jnp.int32, (q, q), 0) >= lax.broadcasted_iota(jnp.int32, (q, q), 1)


def inner_grad_kernel(p, v, g, sl, dl, out):
    n = p.shape[1] // 2
    entry, readout = p[:, :n], p[:, n:]
    scores = jnp.where(causal(p.shape[0]), dot(g[...], v[...], 1, 1), 0.0).astype(bf16)
    out[:, :n] = dot(scores, readout, 0, 0) + dot(v[...], dl[0], 1, 1)
    out[:, n:] = dot(scores, entry, 1, 0) + dot(g[...], sl[0], 1, 1)


def inner_grad(p, v, g, sl, dl):
    t, d = v.shape
    n2 = p.shape[1]
    row = lambda w: pl.BlockSpec((CHUNK, w), lambda i: (i, 0))
    st = pl.BlockSpec((1, n2 // 2, d), lambda i: (i, 0, 0))
    return pl.pallas_call(
        inner_grad_kernel,
        grid=(t // CHUNK,),
        in_specs=[row(n2), row(d), row(d), st, st],
        out_specs=row(n2),
        out_shape=shape((t, n2), f32),
        compiler_params=params(),
        cost_estimate=cost(6 * t * d * CHUNK, 8 * t * d),
        name="inner_grad",
    )(p, v, g, sl, dl)


def outer_grad_kernel(inner, v, g, si, di, half, out, acc):
    t, _ = v.shape
    n = inner.shape[1] // 2
    count = t // CHUNK
    i = pl.program_id(0)

    @pl.when(i == 0)
    def _():
        acc[...] = inner[...]

    carry = jnp.ones(half[0, 0:1, :].shape, f32)
    state = si[0].astype(f32)
    for k in range(count):
        rows = slice(k * CHUNK, (k + 1) * CHUNK)
        hk = half[k, 0:1, :]
        acc[rows, n:] += dot(g[rows, :], (state * (carry * hk)).astype(bf16), 1, 1)
        carry = carry * hk * hk
    carry = jnp.ones(half[0, 0:1, :].shape, f32)
    state = di[0].astype(f32)
    for k in reversed(range(count)):
        rows = slice(k * CHUNK, (k + 1) * CHUNK)
        hk = half[k, 0:1, :]
        acc[rows, :n] += dot(v[rows, :], (state * (carry * hk)).astype(bf16), 1, 1)
        carry = carry * hk * hk

    @pl.when(i == pl.num_programs(0) - 1)
    def _():
        out[...] = acc[...].astype(bf16)


def outer_grad(inner, v, g, si, di, half):
    t, d = v.shape
    n2 = inner.shape[1]
    count = t // CHUNK
    w = d // PIECES
    cols = pl.BlockSpec((t, w), lambda i: (0, i))
    whole = pl.BlockSpec((t, n2), lambda i: (0, 0))
    piece = pl.BlockSpec((1, n2 // 2, w), lambda i: (i, 0, 0))
    return pl.pallas_call(
        outer_grad_kernel,
        grid=(PIECES,),
        in_specs=[whole, cols, cols, piece, piece, pl.BlockSpec((count, 8, w), lambda i: (0, 0, i))],
        out_specs=whole,
        out_shape=shape((t, n2), bf16),
        scratch_shapes=[pltpu.VMEM((t, n2), f32)],
        compiler_params=params(),
        cost_estimate=cost(2 * t * d * n2, 4 * t * d),
        name="outer_grad",
    )(inner, v, g, si, di, half)


def weight_grad_kernel(x, p, out):
    out[...] = dot(x[...], p[...], 0, 0).astype(bf16)


def weight_grad(x, low):
    t, d = x.shape
    n2 = low.shape[1]
    w = d // PIECES
    return pl.pallas_call(
        weight_grad_kernel,
        grid=(PIECES,),
        in_specs=[pl.BlockSpec((t, w), lambda i: (0, i)), pl.BlockSpec((t, n2), lambda i: (0, 0))],
        out_specs=pl.BlockSpec((w, n2), lambda i: (i, 0)),
        out_shape=shape((d, n2), bf16),
        compiler_params=params(),
        cost_estimate=cost(2 * t * d * n2, 2 * t * d),
        name="weight_grad",
    )(x, low)


def finish_kernel(f_ref, *refs, keys, block, first, heads, chained):
    (x, v, g, cot, newest, midcot, p, low, sl, dl, si, di, half, skip, a, b, rstd) = refs[:17]
    refs = refs[17:]
    weights = refs[: len(keys)]
    refs = refs[len(keys) + (2 if chained else 0) :]
    rebuilt_o, grad_o, grad, fcar, bcar = refs
    q, d = x.shape
    n = p.shape[1] // 2
    ps = d // heads
    count = half.shape[0]
    w = d // PIECES
    k = first + pl.program_id(0)
    f = f_ref[0]

    for (key, lo), wt in zip(keys, weights):
        start = pl.multiple_of(jnp.bitwise_xor(f, key) * block + lo, 128)
        grad[:, pl.ds(start, wt.shape[0])] = dot(low[...], wt[...], 1, 1)

    ahead = jnp.ones((1, d), f32)
    behind = jnp.ones((1, d), f32)
    for j in range(count):
        hj = half[j, 0:1, :]
        sq = hj * hj
        ahead = ahead * jnp.where(j < k, sq, jnp.where(j == k, hj, 1.0))
        behind = behind * jnp.where(j > k, sq, jnp.where(j == k, hj, 1.0))
    fcar[...] = jnp.broadcast_to(ahead, fcar.shape)
    bcar[...] = jnp.broadcast_to(behind, bcar.shape)

    entry, readout = p[:, :n], p[:, n:]
    scores = jnp.where(causal(q), dot(readout, entry, 1, 1), 0.0).astype(bf16)
    dots = jnp.zeros((q, 1), f32)
    for i in range(PIECES):
        cols = slice(i * w, (i + 1) * w)
        state = (sl[0, :, cols].astype(f32) + si[i].astype(f32) * fcar[0:1, cols]).astype(bf16)
        mixed = dot(scores, v[:, cols], 1, 0) + dot(readout, state, 1, 0)
        state = (dl[0, :, cols].astype(f32) + di[i].astype(f32) * bcar[0:1, cols]).astype(bf16)
        back = dot(scores, g[:, cols], 0, 0) + dot(entry, state, 1, 0)
        for h in range(w // ps):
            hh = i * (w // ps) + h
            wide = slice(hh * ps, (hh + 1) * ps)
            own = slice(h * ps, (h + 1) * ps)
            xf = x[:, wide].astype(f32)
            sk = skip[0:1, wide]
            y = mixed[:, own] * a[:, hh : hh + 1] + sk * xf
            rebuilt_o[:, wide] = (newest[:, wide].astype(f32) - y).astype(bf16)
            gr = grad[:, wide] + back[:, own] * b[:, hh : hh + 1] + sk * cot[:, wide].astype(f32)
            grad[:, wide] = gr
            dots = dots + jnp.sum(gr * xf, axis=-1, keepdims=True)
    dots = dots * (1.0 / d)
    scale = rstd[...]
    for i in range(PIECES):
        cols = slice(i * w, (i + 1) * w)
        dx = scale * (grad[:, cols] - x[:, cols].astype(f32) * dots)
        grad_o[:, cols] = (midcot[:, cols].astype(f32) + dx).astype(bf16)


def finish(f, x, v, g, cot, newest, midcot, p, low, sl, dl, si, di, half, skip, a, b, rstd,
           keys, pieces, block, first, number, previous):
    t, d = x.shape
    n2 = p.shape[1]
    n = n2 // 2
    heads = a.shape[1]
    count = half.shape[0]
    w = d // PIECES
    row = lambda m: pl.BlockSpec((CHUNK, m), lambda i: (first + i, 0))
    st = pl.BlockSpec((1, n, d), lambda i: (first + i, 0, 0))
    inc = pl.BlockSpec((PIECES, n, w), lambda i: (0, 0, 0))
    const = lambda s: pl.BlockSpec(s, lambda i: (0,) * len(s))
    chained = previous is not None
    in_specs = [pl.BlockSpec(memory_space=pltpu.SMEM), row(d), row(d), row(d), row(d), row(d), row(d),
                row(n2), row(n2), st, st, inc, inc, const((count, 8, d)), const((1, d)), row(heads),
                row(heads), row(1)] + [const(piece.shape) for piece in pieces]
    args = [f, x, v, g, cot, newest, midcot, p, low, sl, dl, si, di, half, skip, a, b, rstd, *pieces]
    aliases = {}
    if chained:
        aliases = {len(args): 0, len(args) + 1: 1}
        args += list(previous)
        in_specs += [pl.BlockSpec(memory_space=pl.ANY)] * 2
    rows = number * CHUNK
    return pl.pallas_call(
        functools.partial(finish_kernel, keys=keys, block=block, first=first, heads=heads, chained=chained),
        grid=(number,),
        in_specs=in_specs,
        out_specs=[row(d), row(d)],
        out_shape=[shape((t, d), bf16)] * 2,
        scratch_shapes=[pltpu.VMEM((CHUNK, d), f32), pltpu.VMEM((8, d), f32), pltpu.VMEM((8, d), f32)],
        input_output_aliases=aliases,
        compiler_params=params(),
        cost_estimate=cost(8 * rows * d * n + 2 * rows * d * n2, 24 * rows * d),
        name=f"finish_{first}",
    )(*args)


def flip(x, bit):
    count = lax.axis_size("fsdp")
    return lax.ppermute(x, "fsdp", [(i, i ^ bit) for i in range(count)])


def gather_weights(w):
    count = lax.axis_size("fsdp")
    rows = w.shape[0]
    if count == 8:
        across, along = flip(w, 2), flip(w, 4)
        mid = rows // 2
        held = [(0, 0, w), (2, 0, across), (4, 0, along),
                (6, 0, flip(across[:mid], 4)), (6, mid, flip(along[mid:], 2))]
        held += [(k | 1, lo, flip(a, 1)) for k, lo, a in held]
    else:
        held = [(0, 0, w)]
        bit = count // 2
        while bit:
            held += [(k | bit, lo, flip(a, bit)) for k, lo, a in held]
            bit //= 2
    return [(k, lo) for k, lo, _ in held], [a for _, _, a in held]


def fold(x, axis, bit):
    mine = (lax.axis_index("fsdp") // bit) % 2
    away = flip(lax.dynamic_index_in_dim(x, 1 - mine, axis, False), bit)
    kept = lax.dynamic_index_in_dim(x, mine, axis, False)
    return (kept.astype(f32) + away.astype(f32)).astype(bf16)


def scatter_sum(partial):
    d, n2 = partial.shape
    along = lax.axis_size("seq")
    count = lax.axis_size("fsdp")
    bits = [1 << i for i in range(count.bit_length() - 1)]
    rows = d // (along * count)
    x = partial.reshape((along,) + (2,) * len(bits) + (rows, n2))
    x = fold(x, len(bits), 1)
    left, right = x[..., : n2 // 2], x[..., n2 // 2 :]
    rest = bits[1:]
    for i, bit in enumerate(rest):
        left = fold(left, len(rest) - i, bit)
    for i, bit in enumerate(reversed(rest)):
        right = fold(right, 1, bit)
    x = jnp.concatenate([left, right], axis=-1)
    z = lax.axis_index("seq")
    total = lax.dynamic_index_in_dim(x, z, 0, False).astype(f32)
    for k in range(1, along):
        block = lax.dynamic_index_in_dim(x, (z + k) % along, 0, False)
        total = total + lax.ppermute(block, "seq", [(i, (i + k) % along) for i in range(along)]).astype(f32)
    return total


def shards(middle_state, newest_state, middle_cotangent, newest_cotangent, log_decay, state_weights, skip_gain):
    t, d = middle_state.shape[1:]
    heads = log_decay.shape[2]
    f = lax.axis_index("fsdp").astype(jnp.int32).reshape(1)
    block = state_weights.shape[0]
    keys, pieces = gather_weights(state_weights)
    x, v, g, rstd, a, b, half = prepare(middle_state[0], newest_cotangent[0], log_decay[0])
    p = project(f, x, keys, pieces, block)
    sl, dl, sloc, dloc, dtot = states(p, v, g, half)
    inner = inner_grad(p, v, g, sl, dl)
    si, di = pass_states(sloc, dloc, dtot)
    low = outer_grad(inner, v, g, si, di, half)
    partial = weight_grad(x, low)
    skip = jnp.repeat(skip_gain, d // heads)[None]
    outs = None
    count = t // CHUNK
    for first in range(0, count, 2):
        outs = finish(f, x, v, g, newest_cotangent[0], newest_state[0], middle_cotangent[0], p, low, sl, dl,
                      si, di, half, skip, a, b, rstd, keys, pieces, block, first, 2, outs)
    summed = scatter_sum(partial)
    scale = (t * lax.axis_size("seq") * lax.axis_size("fsdp")) ** (-0.5)
    return outs[0][None], outs[1][None], summed * scale


def solution(mesh):
    return jax.shard_map(
        shards,
        mesh=mesh,
        in_specs=(
            P("fsdp", "seq", None),
            P("fsdp", "seq", None),
            P("fsdp", "seq", None),
            P("fsdp", "seq", None),
            P("fsdp", "seq", None),
            P("fsdp", None),
            P(),
        ),
        out_specs=(P("fsdp", "seq", None), P("fsdp", "seq", None), P(("seq", "fsdp"), None)),
        check_vma=False,
    )
```

```python
import functools

import jax
import jax.numpy as jnp
from jax import lax
from jax.experimental import pallas as pl
from jax.experimental.pallas import tpu as pltpu
from jax.sharding import PartitionSpec as P


CHUNK = 128
PIECES = 4
MIB = 1024 * 1024

f32 = jnp.float32
bf16 = jnp.bfloat16
norm_epsilon = 1e-05
decay_unit = 1.0 / 4096.0


def dot(a, b, ca, cb):
    return lax.dot_general(a, b, (((ca,), (cb,)), ((), ())), preferred_element_type=f32)


def params(mib):
    return pltpu.CompilerParams(vmem_limit_bytes=mib * MIB)


def cost(flops, nbytes):
    return pl.CostEstimate(flops=int(flops), bytes_accessed=int(nbytes), transcendentals=0)


def shape(s, d):
    return jax.ShapeDtypeStruct(s, d)


def in_hbm(x):
    return pltpu.with_memory_space_constraint(x, pltpu.HBM)


def near(x):
    return pltpu.with_memory_space_constraint(x, pltpu.VMEM)


def kept(s, d):
    return pltpu.VMEM(s, d)


def normalize_kernel(meta, mid, decay, x_o, rstd_o, a_o, b_o, half_o, *, heads):
    del meta
    q, d = mid.shape
    ps = d // heads
    values = mid[...].astype(f32)
    rstd = lax.rsqrt(jnp.mean(values * values, axis=-1, keepdims=True) + norm_epsilon)
    rstd_o[...] = rstd
    x_o[...] = (values * rstd).astype(bf16)
    rates = decay[...].astype(f32)
    running = (
        jnp.dot(causal(q).astype(f32), rates, precision=lax.Precision.HIGHEST, preferred_element_type=f32)
        * decay_unit
    )
    mid_log = 0.5 * running[q - 1 : q, :]
    a_o[...] = jnp.exp(running - mid_log) * (ps ** (-0.5))
    b_o[...] = jnp.exp(mid_log - running) * jnp.sqrt(1.0 - jnp.exp(2.0 * (rates * decay_unit)))
    half = jnp.exp(mid_log)
    for h in range(heads):
        half_o[0, :, h * ps : (h + 1) * ps] = jnp.broadcast_to(half[:, h : h + 1], (8, ps))


def normalize(meta, mid, decay):
    t, d = mid.shape
    heads = decay.shape[1]
    n = t // CHUNK
    row = lambda w: pl.BlockSpec((CHUNK, w), lambda i: (i, 0))
    return pl.pallas_call(
        functools.partial(normalize_kernel, heads=heads),
        grid=(n,),
        in_specs=[pl.BlockSpec(memory_space=pltpu.SMEM), row(d), row(heads)],
        out_specs=[row(d), row(1), row(heads), row(heads), pl.BlockSpec((1, 8, d), lambda i: (i, 0, 0))],
        out_shape=[kept((t, d), bf16), kept((t, 1), f32), kept((t, heads), f32), kept((t, heads), f32),
                   kept((n, 8, d), f32)],
        compiler_params=params(12),
        cost_estimate=cost(30 * t * d, 4 * t * d),
        name="normalize",
    )(meta, in_hbm(mid), decay)


def scale_heads_kernel(x, cot, a, b, v_o, g_o, *, heads):
    ps = x.shape[1] // heads
    for h in range(heads):
        cols = slice(h * ps, (h + 1) * ps)
        v_o[:, cols] = (x[:, cols].astype(f32) * b[:, h : h + 1]).astype(bf16)
        g_o[:, cols] = (cot[:, cols].astype(f32) * a[:, h : h + 1]).astype(bf16)


def scale_heads(x, cot, a, b):
    t, d = x.shape
    heads = a.shape[1]
    row = lambda w: pl.BlockSpec((CHUNK, w), lambda i: (i, 0))
    return pl.pallas_call(
        functools.partial(scale_heads_kernel, heads=heads),
        grid=(t // CHUNK,),
        in_specs=[row(d), row(d), row(heads), row(heads)],
        out_specs=[row(d), row(d)],
        out_shape=[kept((t, d), bf16)] * 2,
        compiler_params=params(12),
        cost_estimate=cost(10 * t * d, 8 * t * d),
        name="scale_heads",
    )(near(x), in_hbm(cot), near(a), near(b))


def project_kernel(meta, x, *refs, keys, block):
    weights, (out, full) = refs[:-2], refs[-2:]
    f = meta[0]
    total = None
    for (k, lo), w in zip(keys, weights):
        start = pl.multiple_of(jnp.bitwise_xor(f, k) * block + lo, 128)
        full[pl.ds(start, w.shape[0]), :] = w[...]
        part = dot(x[:, pl.ds(start, w.shape[0])], w[...], 1, 0)
        total = part if total is None else total + part
    out[...] = total.astype(bf16)


def project(meta, x, keys, pieces, block):
    t, d = x.shape
    n2 = pieces[0].shape[1]
    full = pl.BlockSpec(memory_space=pltpu.VMEM)
    return pl.pallas_call(
        functools.partial(project_kernel, keys=keys, block=block),
        in_specs=[pl.BlockSpec(memory_space=pltpu.SMEM), full] + [full] * len(pieces),
        out_specs=[full, full],
        out_shape=[kept((t, n2), bf16), kept((d, n2), bf16)],
        compiler_params=params(16),
        cost_estimate=cost(2 * t * d * n2, 2 * (t * d + d * n2)),
        name="project",
    )(meta, near(x), *pieces)


def states_kernel(p, v, g, half, sl_o, dl_o, loc_o, dtot_o):
    t, w = v.shape
    n = p.shape[1] // 2
    count = t // CHUNK
    state = jnp.zeros((n, w), f32)
    total = jnp.ones((8, w), f32)
    for k in range(count):
        rows = slice(k * CHUNK, (k + 1) * CHUNK)
        hk = half[k, 0:1, :]
        state = state * hk
        sl_o[k] = state.astype(bf16)
        state = (state + dot(p[rows, :n], v[rows, :], 0, 0)) * hk
        total = total * half[k] * half[k]
    loc_o[0, 0] = state.astype(bf16)
    dtot_o[...] = total
    state = jnp.zeros((n, w), f32)
    for k in reversed(range(count)):
        rows = slice(k * CHUNK, (k + 1) * CHUNK)
        hk = half[k, 0:1, :]
        state = state * hk
        dl_o[k] = state.astype(bf16)
        state = (state + dot(p[rows, n:], g[rows, :], 0, 0)) * hk
    loc_o[1, 0] = state.astype(bf16)


def states(p, v, g, half):
    t, d = v.shape
    n = p.shape[1] // 2
    count = t // CHUNK
    w = d // PIECES
    cols = pl.BlockSpec((t, w), lambda i: (0, i))
    chunked = pl.BlockSpec((count, n, w), lambda i: (0, 0, i))
    piece = pl.BlockSpec((2, 1, n, w), lambda i: (0, i, 0, 0))
    return pl.pallas_call(
        states_kernel,
        grid=(PIECES,),
        in_specs=[pl.BlockSpec((t, 2 * n), lambda i: (0, 0)), cols, cols,
                  pl.BlockSpec((count, 8, w), lambda i: (0, 0, i))],
        out_specs=[chunked, chunked, piece, pl.BlockSpec((8, w), lambda i: (0, i))],
        out_shape=[kept((count, n, d), bf16)] * 2
        + [kept((2, PIECES, n, w), bf16), kept((8, d), f32)],
        compiler_params=params(12),
        cost_estimate=cost(4 * t * d * n, 8 * t * d),
        name="states",
    )(near(p), near(v), near(g), near(half))


def hop_kernel(ids, ra, rb, la, lb, da, db, oa, ob):
    del ids
    oa[...] = (la[0, 0].astype(f32) + da[0:1, :] * rb[...].astype(f32)).astype(bf16)
    ob[...] = (lb[0, 0].astype(f32) + db[0:1, :] * ra[...].astype(f32)).astype(bf16)


def hop(ids, j, ra, rb, loc, dtot):
    n, w = ra.shape
    whole = pl.BlockSpec((n, w), lambda i, s: (0, 0))
    own = lambda c: pl.BlockSpec((1, 1, n, w), lambda i, s: (s[2 + 8 * j + c], s[2 + 8 * j + c + 1], 0, 0))
    dec = lambda c: pl.BlockSpec((8, w), lambda i, s: (0, s[2 + 8 * j + c + 1]))
    return pl.pallas_call(
        hop_kernel,
        grid_spec=pltpu.PrefetchScalarGridSpec(
            num_scalar_prefetch=1,
            grid=(1,),
            in_specs=[whole, whole, own(0), own(2), dec(0), dec(2)],
            out_specs=[whole, whole],
        ),
        out_shape=[shape((n, w), bf16)] * 2,
        compiler_params=params(8),
        cost_estimate=cost(4 * n * w, 12 * n * w),
    )(ids, ra, rb, near(loc), near(loc), near(dtot), near(dtot))


def absorb_kernel(ids, ra, rb, v, g, hf, hb, *refs, j):
    si_o, di_o, acc = refs[-3:]
    t, _ = v.shape
    n = ra.shape[0]
    count = t // CHUNK
    odd = ids[2 + 8 * j] == 1
    zero = jnp.zeros(ra.shape, f32)
    fa = ra[...].astype(f32)
    fb = rb[...].astype(f32)
    ahead = jnp.where(odd, fa, fb)
    behind = jnp.where(odd, fb, fa)
    si_o[0] = ahead.astype(bf16)
    di_o[0] = behind.astype(bf16)
    ahead = jnp.where(ids[2 + 8 * j + 4] == ids[2 + 8 * j + 5], ahead, zero)
    behind = jnp.where(ids[2 + 8 * j + 6] == ids[2 + 8 * j + 7], behind, zero)
    carry = jnp.ones(hf[0, 0:1, :].shape, f32)
    for k in range(count):
        rows = slice(k * CHUNK, (k + 1) * CHUNK)
        hk = hf[k, 0:1, :]
        part = dot(g[rows, :], (ahead * (carry * hk)).astype(bf16), 1, 1)
        acc[rows, n:] = part if len(refs) == 5 else refs[2][rows, n:] + part
        carry = carry * hk * hk
    carry = jnp.ones(hf[0, 0:1, :].shape, f32)
    for k in reversed(range(count)):
        rows = slice(k * CHUNK, (k + 1) * CHUNK)
        hk = hb[k, 0:1, :]
        part = dot(v[rows, :], (behind * (carry * hk)).astype(bf16), 1, 1)
        acc[rows, :n] = part if len(refs) == 5 else refs[2][rows, :n] + part
        carry = carry * hk * hk


def absorb(ids, j, ra, rb, v, g, half, si, di, acc):
    t, _ = v.shape
    n, w = ra.shape
    count = t // CHUNK
    whole = lambda *s: pl.BlockSpec(s, lambda i, q: (0,) * len(s))
    cols = lambda c: pl.BlockSpec((t, w), lambda i, q: (0, q[2 + 8 * j + c]))
    dec = lambda c: pl.BlockSpec((count, 8, w), lambda i, q: (0, 0, q[2 + 8 * j + c]))
    slot = lambda c: pl.BlockSpec((1, n, w), lambda i, q: (q[2 + 8 * j + c], 0, 0))
    anyspace = pl.BlockSpec(memory_space=pl.ANY)
    args = [ids, ra, rb, near(v), near(g), near(half), near(half), si, di]
    in_specs = [whole(n, w), whole(n, w), cols(6), cols(4), dec(4), dec(6), anyspace, anyspace]
    if acc is not None:
        args.append(near(acc))
        in_specs.append(whole(t, 2 * n))
    return pl.pallas_call(
        functools.partial(absorb_kernel, j=j),
        grid_spec=pltpu.PrefetchScalarGridSpec(
            num_scalar_prefetch=1,
            grid=(1,),
            in_specs=in_specs,
            out_specs=[slot(5), slot(7), whole(t, 2 * n)],
        ),
        out_shape=[shape(si.shape, bf16), shape(di.shape, bf16), kept((t, 2 * n), f32)],
        input_output_aliases={7: 0, 8: 1},
        compiler_params=params(8),
        cost_estimate=cost(4 * t * w * n, 4 * t * w),
    )(*args)


def pick_kernel(ids, la, lb, oa, ob):
    del ids
    oa[...] = la[0, 0]
    ob[...] = lb[0, 0]


def pick(ids, loc):
    _, _, n, w = loc.shape
    whole = pl.BlockSpec((n, w), lambda i, s: (0, 0))
    own = lambda c: pl.BlockSpec((1, 1, n, w), lambda i, s: (s[2 + c], s[3 + c], 0, 0))
    return pl.pallas_call(
        pick_kernel,
        grid_spec=pltpu.PrefetchScalarGridSpec(
            num_scalar_prefetch=1, grid=(1,), in_specs=[own(0), own(2)], out_specs=[whole, whole]),
        out_shape=[shape((n, w), bf16)] * 2,
        compiler_params=params(8),
        cost_estimate=cost(0, 8 * n * w),
        name="pick",
    )(ids, near(loc), near(loc))


def places():
    count = lax.axis_size("seq")
    z = lax.axis_index("seq")
    j = jnp.arange(PIECES + count - 2, dtype=jnp.int32)
    odd = jnp.zeros_like(j) + z % 2
    clip = lambda at: jnp.clip(at, 0, PIECES - 1)
    slot = lambda at: jnp.where((at >= 0) & (at < PIECES), at, PIECES)
    ahead, behind = j - z, j - (count - 1 - z)
    first = jnp.where(odd == 1, behind, ahead)
    second = jnp.where(odd == 1, ahead, behind)
    ids = jnp.stack(
        [odd, clip(first), 1 - odd, clip(second),
         clip(ahead + 1), slot(ahead + 1), clip(behind + 1), slot(behind + 1)], axis=1).reshape(-1)
    own = jnp.stack([lax.axis_index("fsdp"), z]).astype(jnp.int32)
    return jnp.concatenate([own, ids])


def pass_states(ids, loc, dtot, v, g, half):
    count = lax.axis_size("seq")
    _, _, n, w = loc.shape
    steps = PIECES + count - 2
    pairs_a = [(i, i ^ 1) for i in range(count) if i ^ 1 < count]
    pairs_b = [p for i in range(1, count - 1, 2) for p in ((i, i + 1), (i + 1, i))]
    si = jnp.zeros((PIECES + 1, n, w), bf16)
    di = jnp.zeros((PIECES + 1, n, w), bf16)
    acc = None
    done = []
    for step in range(steps):
        if step == 0:
            sa, sb = pick(ids, loc)
        else:
            sa, sb = hop(ids, step, ra, rb, loc, dtot)
        ra = lax.ppermute(sa, "seq", pairs_a)
        rb = lax.ppermute(sb, "seq", pairs_b)
        si, di, acc = absorb(ids, step, ra, rb, v, g, half, si, di, acc)
        if step >= count - 2:
            done.append((si, di))
    return acc, done


def causal(q):
    return lax.broadcasted_iota(jnp.int32, (q, q), 0) >= lax.broadcasted_iota(jnp.int32, (q, q), 1)


def inner_grad_kernel(p, v, g, sl, dl, out):
    n = p.shape[1] // 2
    entry, readout = p[:, :n], p[:, n:]
    scores = jnp.where(causal(p.shape[0]), dot(g[...], v[...], 1, 1), 0.0).astype(bf16)
    out[:, :n] = dot(scores, readout, 0, 0) + dot(v[...], dl[0], 1, 1)
    out[:, n:] = dot(scores, entry, 1, 0) + dot(g[...], sl[0], 1, 1)


def inner_grad(p, v, g, sl, dl, k):
    _, d = v.shape
    n2 = p.shape[1]
    row = lambda w: pl.BlockSpec((CHUNK, w), lambda i: (k, 0))
    st = pl.BlockSpec((1, n2 // 2, d), lambda i: (k, 0, 0))
    return pl.pallas_call(
        inner_grad_kernel,
        grid=(1,),
        in_specs=[row(n2), row(d), row(d), st, st],
        out_specs=pl.BlockSpec((CHUNK, n2), lambda i: (0, 0)),
        out_shape=kept((CHUNK, n2), f32),
        compiler_params=params(12),
        cost_estimate=cost(6 * CHUNK * d * CHUNK, 8 * CHUNK * d),
    )(near(p), near(v), near(g), near(sl), near(dl))


def weight_grad_kernel(meta, x, acc, *refs):
    inner, (away, kept_o, low_o, low, term) = refs[:-5], refs[-5:]

    @pl.when(pl.program_id(0) == 0)
    def _():
        for k, part in enumerate(inner):
            rows = slice(k * CHUNK, (k + 1) * CHUNK)
            low[rows, :] = (acc[rows, :] + part[...]).astype(bf16)
        low_o[...] = low[...]

    term[...] = dot(x[...], low[...], 0, 0)
    _, half, rows, _ = away.shape
    mine = lax.rem(meta[0], 2)
    for i in range(half):
        start = pl.multiple_of((2 * i + mine) * rows, 8)
        kept_o[0, i] = term[pl.ds(start, rows), :].astype(bf16)
        start = pl.multiple_of((2 * i + 1 - mine) * rows, 8)
        away[0, i] = term[pl.ds(start, rows), :].astype(bf16)


def weight_grad(meta, x, acc, inner):
    t, d = x.shape
    n2 = acc.shape[1]
    along, count = lax.axis_size("seq"), lax.axis_size("fsdp")
    w = d // along
    whole = lambda r: pl.BlockSpec((r, n2), lambda i: (0, 0))
    blocks = (along, count // 2, w // count, n2)
    split = pl.BlockSpec((1,) + blocks[1:], lambda i: (i, 0, 0, 0))
    return pl.pallas_call(
        weight_grad_kernel,
        grid=(along,),
        in_specs=[pl.BlockSpec(memory_space=pltpu.SMEM), pl.BlockSpec((t, w), lambda i: (0, i)), whole(t)]
        + [whole(CHUNK)] * len(inner),
        out_specs=[split, split, whole(t)],
        out_shape=[shape(blocks, bf16), kept(blocks, bf16), kept((t, n2), bf16)],
        scratch_shapes=[pltpu.VMEM((t, n2), bf16), pltpu.VMEM((w, n2), f32)],
        compiler_params=params(12),
        cost_estimate=cost(2 * t * d * n2, 2 * t * d),
        name="weight_grad",
    )(meta, near(x), near(acc), *map(near, inner))


def piece_kernel(x, v, g, cot, newest, p, sl, dl, si, di, half, skip, a, b, *refs, piece, ps):
    rebuilt_o, back_o = refs[-2:]
    w = x.shape[1]
    n = p.shape[1] // 2
    per = w // ps
    k = pl.program_id(0)
    ahead = jnp.ones((1, w), f32)
    behind = ahead
    for j in range(half.shape[0]):
        hj = half[j, 0:1, :]
        sq = hj * hj
        own = jnp.where(j == k, hj, 1.0)
        ahead = ahead * jnp.where(j < k, sq, own)
        behind = behind * jnp.where(j > k, sq, own)
    entry, readout = p[:, :n], p[:, n:]
    scores = jnp.where(causal(CHUNK), dot(readout, entry, 1, 1), 0.0).astype(bf16)
    state = (sl[0].astype(f32) + si[0].astype(f32) * ahead).astype(bf16)
    mixed = dot(scores, v[...], 1, 0) + dot(readout, state, 1, 0)
    state = (dl[0].astype(f32) + di[0].astype(f32) * behind).astype(bf16)
    back = dot(scores, g[...], 0, 0) + dot(entry, state, 1, 0)
    for h in range(per):
        hh = piece * per + h
        own = slice(h * ps, (h + 1) * ps)
        sk = skip[0:1, own]
        y = mixed[:, own] * a[:, hh : hh + 1] + sk * x[:, own].astype(f32)
        rebuilt_o[:, own] = (newest[:, own].astype(f32) - y).astype(bf16)
        gr = back[:, own] * b[:, hh : hh + 1] + sk * cot[:, own].astype(f32)
        back_o[:, own] = gr.astype(bf16)


def state_piece(x, v, g, cot, newest, p, sl, dl, si, di, half, skip, a, b, piece, previous):
    t, d = x.shape
    n2 = p.shape[1]
    n = n2 // 2
    heads = a.shape[1]
    count = half.shape[0]
    w = d // PIECES
    cols = pl.BlockSpec((CHUNK, w), lambda i: (i, piece))
    chunked = pl.BlockSpec((1, n, w), lambda i: (i, 0, piece))
    inc = pl.BlockSpec((1, n, w), lambda i: (piece, 0, 0))
    row = lambda m: pl.BlockSpec((CHUNK, m), lambda i: (i, 0))
    args = [near(x), near(v), near(g), in_hbm(cot), in_hbm(newest), near(p), near(sl), near(dl), si, di, near(half),
            skip, near(a), near(b)]
    in_specs = [cols] * 5 + [row(n2), chunked, chunked, inc, inc,
                             pl.BlockSpec((count, 8, w), lambda i: (0, 0, piece)),
                             pl.BlockSpec((1, w), lambda i: (0, piece)), row(heads), row(heads)]
    aliases = {}
    if previous is not None:
        aliases = {len(args): 0}
        args.append(previous)
        in_specs.append(pl.BlockSpec(memory_space=pltpu.HBM))
    return pl.pallas_call(
        functools.partial(piece_kernel, piece=piece, ps=d // heads),
        grid=(t // CHUNK,),
        in_specs=in_specs,
        out_specs=[cols, pl.BlockSpec((CHUNK, w), lambda i: (i, 0))],
        out_shape=[pltpu.HBM((t, d), bf16), kept((t, w), bf16)],
        input_output_aliases=aliases,
        compiler_params=params(10),
        cost_estimate=cost(8 * t * w * n, 18 * t * w),
    )(*args)


def finish_kernel(x, midcot, low, rstd, weights, *refs):
    backs = refs[:PIECES]
    grad_o, grad = refs[-2:]
    d = x.shape[1]
    grad[...] = dot(low[...], weights[...], 1, 1)
    w = d // PIECES
    dots = jnp.zeros((x.shape[0], 1), f32)
    for i, back in enumerate(backs):
        cols = slice(i * w, (i + 1) * w)
        gr = grad[:, cols] + back[...].astype(f32)
        grad[:, cols] = gr
        dots = dots + jnp.sum(gr * x[:, cols].astype(f32), axis=-1, keepdims=True)
    scale = rstd[...]
    dots = dots * (scale * (1.0 / d))
    for i in range(PIECES):
        cols = slice(i * w, (i + 1) * w)
        dx = scale * grad[:, cols] - x[:, cols].astype(f32) * dots
        grad_o[:, cols] = (midcot[:, cols].astype(f32) + dx).astype(bf16)


def finish(x, backs, midcot, low, rstd, weights, first, number, previous):
    t, d = x.shape
    n2 = low.shape[1]
    row = lambda m: pl.BlockSpec((CHUNK, m), lambda i: (first + i, 0))
    args = [near(x), in_hbm(midcot), near(low), near(rstd), near(weights), *map(near, backs)]
    in_specs = [row(d), row(d), row(n2), row(1), pl.BlockSpec(memory_space=pltpu.VMEM)] + [row(d // PIECES)] * PIECES
    aliases = {}
    if previous is not None:
        aliases = {len(args): 0}
        args.append(previous)
        in_specs.append(pl.BlockSpec(memory_space=pltpu.HBM))
    return pl.pallas_call(
        finish_kernel,
        grid=(number,),
        in_specs=in_specs,
        out_specs=row(d),
        out_shape=pltpu.HBM((t, d), bf16),
        scratch_shapes=[pltpu.VMEM((CHUNK, d), f32)],
        input_output_aliases=aliases,
        compiler_params=params(16),
        cost_estimate=cost(2 * number * CHUNK * d * n2, 8 * number * CHUNK * d),
    )(*args)


def flip(x, bit):
    count = lax.axis_size("fsdp")
    return lax.ppermute(x, "fsdp", [(i, i ^ bit) for i in range(count)])


def gather_weights(w):
    count = lax.axis_size("fsdp")
    rows = w.shape[0]
    if count == 8:
        across, along = flip(w, 2), flip(w, 4)
        mid = rows // 2
        held = [(0, 0, w), (2, 0, across), (4, 0, along),
                (6, 0, flip(across[:mid], 4)), (6, mid, flip(along[mid:], 2))]
        held += [(k | 1, lo, flip(a, 1)) for k, lo, a in held]
    else:
        held = [(0, 0, w)]
        bit = count // 2
        while bit:
            held += [(k | bit, lo, flip(a, bit)) for k, lo, a in held]
            bit //= 2
    return [(k, lo) for k, lo, _ in held], [a for _, _, a in held]


def halve(value, away, kept_o, mine, pos):
    low = 1 << pos
    for i in range(away.shape[1]):
        base = (i // low) * 2 * low + i % low
        kept_o[:, i] = value(base + mine * low)
        away[:, i] = value(base + (1 - mine) * low)


def fold_kernel(meta, *refs, first, left, right):
    f = meta[0]
    bit = lambda b: lax.rem(lax.div(f, b), 2)
    pos = lambda b, order: sorted(order).index(b)
    if first:
        kept_i, got, al, kl, ar, kr, total = refs
        total[...] = (kept_i[...].astype(f32) + got[...].astype(f32)).astype(bf16)
        n = al.shape[-1]
        halve(lambda m: total[:, m, :, :n], al, kl, bit(left[0]), pos(left[0], left))
        halve(lambda m: total[:, m, :, n:], ar, kr, bit(right[0]), pos(right[0], right))
        return
    kl, gl, kr, gr, al_o, kl_o, ar_o, kr_o, tl, tr = refs
    tl[...] = (kl[...].astype(f32) + gl[...].astype(f32)).astype(bf16)
    tr[...] = (kr[...].astype(f32) + gr[...].astype(f32)).astype(bf16)
    halve(lambda m: tl[:, m], al_o, kl_o, bit(left[0]), pos(left[0], left))
    halve(lambda m: tr[:, m], ar_o, kr_o, bit(right[0]), pos(right[0], right))


def fold(meta, arrays, left, right, first):
    along, blocks, rows, n = arrays[0].shape
    n = n // 2 if first else n
    out = (along, blocks // 2, rows, n)
    vmem = pl.BlockSpec(memory_space=pltpu.VMEM)
    scratch = [pltpu.VMEM(arrays[0].shape, bf16)] * (1 if first else 2)
    return pl.pallas_call(
        functools.partial(fold_kernel, first=first, left=left, right=right),
        in_specs=[pl.BlockSpec(memory_space=pltpu.SMEM)] + [vmem] * len(arrays),
        out_specs=[vmem] * 4,
        out_shape=[shape(out, bf16), kept(out, bf16)] * 2,
        scratch_shapes=scratch,
        compiler_params=params(10),
        cost_estimate=cost(0, 8 * along * blocks * rows * n),
    )(meta, *arrays)


def deal_kernel(meta, kl, gl, kr, gr, own, *refs):
    along, _, _, n = kl.shape
    sends, both = refs[:-1], refs[-1]
    z = meta[1]
    both[:, :, :n] = (kl[:, 0].astype(f32) + gl[:, 0].astype(f32)).astype(bf16)
    both[:, :, n:] = (kr[:, 0].astype(f32) + gr[:, 0].astype(f32)).astype(bf16)
    own[...] = both[z]
    for k, out in enumerate(sends, 1):
        out[...] = both[lax.rem(z + k, along)]


def deal(meta, arrays):
    along, _, rows, n = arrays[0].shape
    vmem = pl.BlockSpec(memory_space=pltpu.VMEM)
    return pl.pallas_call(
        deal_kernel,
        in_specs=[pl.BlockSpec(memory_space=pltpu.SMEM)] + [vmem] * 4,
        out_specs=[vmem] * along,
        out_shape=[shape((rows, 2 * n), bf16)] * along,
        scratch_shapes=[pltpu.VMEM((along, rows, 2 * n), bf16)],
        compiler_params=params(8),
        cost_estimate=cost(0, 8 * along * rows * n),
        name="deal",
    )(meta, *arrays)


def scatter_sum(meta, away, kept_i):
    along = lax.axis_size("seq")
    count = lax.axis_size("fsdp")
    left = [1 << i for i in range(1, count.bit_length() - 1)]
    right = left[::-1]
    got = flip(away, 1)
    al, kl, ar, kr = fold(meta, [kept_i, got], left, right, True)
    for _ in range(len(left)):
        gl, gr = flip(al, left[0]), flip(ar, right[0])
        left, right = left[1:], right[1:]
        if left:
            al, kl, ar, kr = fold(meta, [kl, gl, kr, gr], left, right, False)
    own, *sends = deal(meta, [kl, gl, kr, gr])
    total = own.astype(f32)
    for k, block in enumerate(sends, 1):
        other = lax.ppermute(block, "seq", [(i, (i + k) % along) for i in range(along)])
        total = total + other.astype(f32)
    return total


def step(middle_state, newest_state, middle_cotangent, newest_cotangent, log_decay, state_weights, skip_gain):
    t, d = middle_state.shape[1:]
    heads = log_decay.shape[2]
    middle, newest, midcot, cot = middle_state[0], newest_state[0], middle_cotangent[0], newest_cotangent[0]
    meta = places()
    block = state_weights.shape[0]
    count = t // CHUNK
    keys, pieces = gather_weights(state_weights)
    x, rstd, a, b, half = normalize(meta, middle, log_decay[0])
    v, g = scale_heads(x, cot, a, b)
    p, weights = project(meta, x, keys, pieces, block)
    sl, dl, loc, dtot = states(p, v, g, half)
    inner = [inner_grad(p, v, g, sl, dl, k) for k in range(count)]
    acc, heads_done = pass_states(meta, loc, dtot, v, g, half)
    away, stays, low = weight_grad(meta, x, acc, inner)
    skip = jnp.repeat(skip_gain, d // heads)[None]
    rebuilt, backs = None, []
    for i in range(PIECES):
        sp, dp = heads_done[i]
        rebuilt, back = state_piece(
            x, v, g, cot, newest, p, sl, dl, sp, dp, half, skip, a, b, i, rebuilt)
        backs.append(back)
    gradient = None
    for i in range(2):
        gradient = finish(x, backs, midcot, low, rstd, weights,
                          i * count // 2, count // 2, gradient)
    summed = scatter_sum(meta, away, stays)
    scale = (t * lax.axis_size("seq") * lax.axis_size("fsdp")) ** (-0.5)
    return rebuilt[None], gradient[None], summed * scale


def solution(mesh):
    whole = P("fsdp", "seq", None)
    return jax.shard_map(
        step,
        mesh=mesh,
        in_specs=(whole, whole, whole, whole, whole, P("fsdp", None), P()),
        out_specs=(whole, whole, P(("seq", "fsdp"), None)),
        check_vma=False,
    )
```

```python
import functools

import jax
import jax.numpy as jnp
from jax import lax
from jax.experimental import pallas as pl
from jax.experimental.pallas import tpu as pltpu
from jax.sharding import PartitionSpec as P


CHUNK = 128
PIECES = 4
MIB = 1024 * 1024

f32 = jnp.float32
bf16 = jnp.bfloat16
norm_epsilon = 1e-05
decay_unit = 1.0 / 4096.0


def dot(a, b, ca, cb):
    return lax.dot_general(a, b, (((ca,), (cb,)), ((), ())), preferred_element_type=f32)


def params(mib):
    return pltpu.CompilerParams(vmem_limit_bytes=mib * MIB)


def cost(flops, nbytes):
    return pl.CostEstimate(flops=int(flops), bytes_accessed=int(nbytes), transcendentals=0)


def shape(s, d):
    return jax.ShapeDtypeStruct(s, d)


def near(x):
    return pltpu.with_memory_space_constraint(x, pltpu.VMEM)


def kept(s, d):
    return pltpu.VMEM(s, d)


def span(i, n):
    return pl.ds(pl.multiple_of(i * n, n), n)


VM = pl.BlockSpec(memory_space=pltpu.VMEM)
SM = pl.BlockSpec(memory_space=pltpu.SMEM)


def normalize_kernel(meta, mid, decay, x_o, rstd_o, a_o, b_o, half_o, *, heads):
    del meta
    q, d = CHUNK, mid.shape[1]
    ps = d // heads
    own = span(pl.program_id(0), q)
    values = mid[own, :].astype(f32)
    rstd = lax.rsqrt(jnp.mean(values * values, axis=-1, keepdims=True) + norm_epsilon)
    i = pl.program_id(0)
    rstd_o[own, :] = rstd
    x_o[own, :] = (values * rstd).astype(bf16)
    rates = decay[...].astype(f32)
    running = (
        jnp.dot(causal(q).astype(f32), rates, precision=lax.Precision.HIGHEST, preferred_element_type=f32)
        * decay_unit
    )
    mid_log = 0.5 * running[q - 1 : q, :]
    a_o[own, :] = jnp.exp(running - mid_log) * (ps ** (-0.5))
    b_o[own, :] = jnp.exp(mid_log - running) * jnp.sqrt(1.0 - jnp.exp(2.0 * (rates * decay_unit)))
    half = jnp.exp(mid_log)
    for h in range(heads):
        half_o[i, :, h * ps : (h + 1) * ps] = jnp.broadcast_to(half[:, h : h + 1], (8, ps))


def normalize(meta, mid, decay):
    t, d = mid.shape
    heads = decay.shape[1]
    n = t // CHUNK
    row = lambda w: pl.BlockSpec((CHUNK, w), lambda i: (i, 0))
    return pl.pallas_call(
        functools.partial(normalize_kernel, heads=heads),
        grid=(n,),
        in_specs=[SM, VM, row(heads)],
        out_specs=[VM] * 5,
        out_shape=[kept((t, d), bf16), kept((t, 1), f32), kept((t, heads), f32), kept((t, heads), f32),
                   kept((n, 8, d), f32)],
        compiler_params=params(12),
        cost_estimate=cost(30 * t * d, 4 * t * d),
        name="normalize",
    )(meta, near(mid), decay)


def scale_heads_kernel(x, cot, a, b, v_o, g_o, spread):
    q, d = CHUNK, cot.shape[1]
    heads = a.shape[1]
    ps = d // heads
    i = pl.program_id(0)

    @pl.when(i == 0)
    def _():
        head = lax.rem(lax.broadcasted_iota(jnp.int32, spread.shape, 0), heads)
        col = lax.div(lax.broadcasted_iota(jnp.int32, spread.shape, 1), ps)
        spread[...] = jnp.where(head == col, 1.0, 0.0).astype(bf16)

    own = span(i, q)
    both = jnp.concatenate([a[own, :], b[own, :]], axis=0)
    high = both.astype(bf16)
    low = (both - high.astype(f32)).astype(bf16)
    parts = jnp.concatenate([high, low], axis=1)
    w = 4 * ps
    for c in range(d // w):
        cols = slice(c * w, (c + 1) * w)
        wide = dot(parts, spread[:, cols], 1, 0)
        v_o[own, cols] = (x[own, cols].astype(f32) * wide[q:]).astype(bf16)
        g_o[own, cols] = (cot[own, cols].astype(f32) * wide[:q]).astype(bf16)


def scale_heads(x, cot, a, b):
    t, d = x.shape
    return pl.pallas_call(
        scale_heads_kernel,
        grid=(t // CHUNK,),
        in_specs=[VM] * 4,
        out_specs=[VM, VM],
        out_shape=[kept((t, d), bf16)] * 2,
        scratch_shapes=[pltpu.VMEM((2 * a.shape[1], d), bf16)],
        compiler_params=params(8),
        cost_estimate=cost(10 * t * d, 8 * t * d),
        name="scale_heads",
    )(near(x), near(cot), near(a), near(b))


def project_kernel(meta, x, *refs, keys, block):
    weights, (out, full) = refs[:-2], refs[-2:]
    f = meta[0]
    total = None
    for (k, lo), w in zip(keys, weights):
        start = pl.multiple_of(jnp.bitwise_xor(f, k) * block + lo, 128)
        full[pl.ds(start, w.shape[0]), :] = w[...]
        part = dot(x[:, pl.ds(start, w.shape[0])], w[...], 1, 0)
        total = part if total is None else total + part
    out[...] = total.astype(bf16)


def project(meta, x, keys, pieces, block):
    t, d = x.shape
    n2 = pieces[0].shape[1]
    full = pl.BlockSpec(memory_space=pltpu.VMEM)
    return pl.pallas_call(
        functools.partial(project_kernel, keys=keys, block=block),
        in_specs=[pl.BlockSpec(memory_space=pltpu.SMEM), full] + [full] * len(pieces),
        out_specs=[full, full],
        out_shape=[kept((t, n2), bf16), kept((d, n2), bf16)],
        compiler_params=params(16),
        cost_estimate=cost(2 * t * d * n2, 2 * (t * d + d * n2)),
        name="project",
    )(meta, near(x), *pieces)


def states_kernel(meta, p, v, g, half, *refs, first, pieces):
    sl_o, dl_o, loc_o, dtot_o = refs[:4] if first else refs[-4:]
    t, d = v.shape
    w = d // PIECES
    n = p.shape[1] // 2
    count = t // CHUNK
    for at, piece in enumerate(pieces):
        cols = slice(piece * w, (piece + 1) * w)
        here = slice(at * w, (at + 1) * w)
        state = jnp.zeros((n, w), f32)
        total = jnp.ones((8, w), f32)
        for k in range(count):
            rows = slice(k * CHUNK, (k + 1) * CHUNK)
            hk = half[k, 0:1, cols]
            state = state * hk
            sl_o[k, :, here] = state.astype(bf16)
            state = (state + dot(p[rows, :n], v[rows, cols], 0, 0)) * hk
            total = total * half[k, :, cols] * half[k, :, cols]
        onward = state
        loc_o[0, piece] = onward.astype(bf16)
        dtot_o[:, cols] = total
        state = jnp.zeros((n, w), f32)
        for k in reversed(range(count)):
            rows = slice(k * CHUNK, (k + 1) * CHUNK)
            hk = half[k, 0:1, cols]
            state = state * hk
            dl_o[k, :, here] = state.astype(bf16)
            state = (state + dot(p[rows, n:], g[rows, cols], 0, 0)) * hk
        loc_o[1, piece] = state.astype(bf16)
        if first:
            oa, ob = refs[4:]
            odd = meta[2] == 1
            oa[...] = jnp.where(odd, state, onward).astype(bf16)
            ob[...] = jnp.where(odd, onward, state).astype(bf16)


def states(meta, p, v, g, half, previous):
    t, d = v.shape
    n = p.shape[1] // 2
    count = t // CHUNK
    w = d // PIECES
    first = previous is None
    pieces = range(1) if first else range(1, PIECES)
    number = len(pieces)
    args = [meta, near(p), near(v), near(g), near(half)]
    out_shape = [kept((count, n, number * w), bf16)] * 2 + [kept((2, PIECES, n, w), bf16), kept((8, d), f32)]
    aliases = {}
    if first:
        out_shape += [shape((n, w), bf16)] * 2
    else:
        aliases = {5: 2, 6: 3}
        args += [near(previous[0]), near(previous[1])]
    return pl.pallas_call(
        functools.partial(states_kernel, first=first, pieces=pieces),
        in_specs=[SM] + [VM] * (len(args) - 1),
        out_specs=[VM] * len(out_shape),
        out_shape=out_shape,
        input_output_aliases=aliases,
        compiler_params=params(8),
        cost_estimate=cost(4 * t * w * n * number, 8 * t * w * number),
    )(*args)


def hop_kernel(ids, ra, rb, loc, dtot, oa, ob, *, j):
    w = ra.shape[1]
    base = 2 + 8 * j
    for c, came, out in ((0, rb, oa), (2, ra, ob)):
        at = ids[base + c + 1]
        decay = dtot[0:1, span(at, w)]
        out[...] = (loc[ids[base + c], at].astype(f32) + decay * came[...].astype(f32)).astype(bf16)


def hop(ids, j, ra, rb, loc, dtot):
    n, w = ra.shape
    return pl.pallas_call(
        functools.partial(hop_kernel, j=j),
        in_specs=[SM] + [VM] * 4,
        out_specs=[VM, VM],
        out_shape=[shape((n, w), bf16)] * 2,
        compiler_params=params(4),
        cost_estimate=cost(4 * n * w, 12 * n * w),
    )(ids, ra, rb, near(loc), near(dtot))


def absorb_kernel(ids, ra, rb, v, g, half, *refs, j, fresh):
    si_o, di_o, acc = refs[-3:]
    t = v.shape[0]
    n, w = ra.shape
    count = t // CHUNK
    base = 2 + 8 * j
    odd = ids[base] == 1
    fa = ra[...].astype(f32)
    fb = rb[...].astype(f32)
    ahead = jnp.where(odd, fa, fb)
    behind = jnp.where(odd, fb, fa)
    if fresh:
        si_o[...] = jnp.zeros_like(si_o)
        di_o[...] = jnp.zeros_like(di_o)
        acc[...] = jnp.zeros_like(acc)
    si_o[ids[base + 5]] = ahead.astype(bf16)
    di_o[ids[base + 7]] = behind.astype(bf16)
    for c, state, order, other, part in ((4, ahead, range(count), g, slice(n, 2 * n)),
                                         (6, behind, reversed(range(count)), v, slice(0, n))):
        at = ids[base + c]

        @pl.when(at == ids[base + c + 1])
        def _():
            cols = span(at, w)
            carry = jnp.ones((1, w), f32)
            for k in order:
                rows = slice(k * CHUNK, (k + 1) * CHUNK)
                hk = half[k, 0:1, cols]
                acc[rows, part] += dot(other[rows, cols], (state * (carry * hk)).astype(bf16), 1, 1)
                carry = carry * hk * hk


def absorb(ids, j, ra, rb, v, g, half, held):
    t, _ = v.shape
    n, w = ra.shape
    args = [ids, ra, rb, near(v), near(g), near(half)]
    aliases = {}
    if held is not None:
        aliases = {6: 0, 7: 1, 8: 2}
        args += map(near, held)
    return pl.pallas_call(
        functools.partial(absorb_kernel, j=j, fresh=held is None),
        in_specs=[SM] + [VM] * (len(args) - 1),
        out_specs=[VM] * 3,
        out_shape=[kept((PIECES + 1, n, w), bf16)] * 2 + [kept((t, 2 * n), f32)],
        input_output_aliases=aliases,
        compiler_params=params(6),
        cost_estimate=cost(4 * t * w * n, 4 * t * w),
    )(*args)


def places():
    count = lax.axis_size("seq")
    z = lax.axis_index("seq")
    j = jnp.arange(PIECES + count - 2, dtype=jnp.int32)
    odd = jnp.zeros_like(j) + z % 2
    clip = lambda at: jnp.clip(at, 0, PIECES - 1)
    slot = lambda at: jnp.where((at >= 0) & (at < PIECES), at, PIECES)
    ahead, behind = j - z, j - (count - 1 - z)
    first = jnp.where(odd == 1, behind, ahead)
    second = jnp.where(odd == 1, ahead, behind)
    ids = jnp.stack(
        [odd, clip(first), 1 - odd, clip(second),
         clip(ahead + 1), slot(ahead + 1), clip(behind + 1), slot(behind + 1)], axis=1).reshape(-1)
    own = jnp.stack([lax.axis_index("fsdp"), z]).astype(jnp.int32)
    return jnp.concatenate([own, ids])


def pass_states(ids, sa, sb, loc, dtot, v, g, half):
    count = lax.axis_size("seq")
    steps = PIECES + count - 2
    pairs_a = [(i, i ^ 1) for i in range(count) if i ^ 1 < count]
    pairs_b = [p for i in range(1, count - 1, 2) for p in ((i, i + 1), (i + 1, i))]
    held = None
    done = []
    for step in range(steps):
        if step:
            sa, sb = hop(ids, step, ra, rb, loc, dtot)
        ra = lax.ppermute(sa, "seq", pairs_a)
        rb = lax.ppermute(sb, "seq", pairs_b)
        held = absorb(ids, step, ra, rb, v, g, half, held)
        if step >= count - 2:
            done.append(held[:2])
    return held[2], done


def causal(q):
    return lax.broadcasted_iota(jnp.int32, (q, q), 0) >= lax.broadcasted_iota(jnp.int32, (q, q), 1)


def inner_grad_kernel(p, v, g, sa, da, sb, db, out, *, k):
    n = p.shape[1] // 2
    w = sa.shape[2]
    rows = slice(k * CHUNK, (k + 1) * CHUNK)
    entry, readout = p[rows, :n], p[rows, n:]
    scores = jnp.where(causal(CHUNK), dot(g[rows, :], v[rows, :], 1, 1), 0.0).astype(bf16)
    out[:, :n] = dot(scores, readout, 0, 0) + dot(v[rows, :w], da[k], 1, 1) + dot(v[rows, w:], db[k], 1, 1)
    out[:, n:] = dot(scores, entry, 1, 0) + dot(g[rows, :w], sa[k], 1, 1) + dot(g[rows, w:], sb[k], 1, 1)


def inner_grad(p, v, g, sa, da, sb, db, k):
    _, d = v.shape
    n2 = p.shape[1]
    return pl.pallas_call(
        functools.partial(inner_grad_kernel, k=k),
        in_specs=[VM] * 7,
        out_specs=VM,
        out_shape=kept((CHUNK, n2), f32),
        compiler_params=params(6),
        cost_estimate=cost(6 * CHUNK * d * CHUNK, 8 * CHUNK * d),
    )(*map(near, (p, v, g, sa, da, sb, db)))


def weight_grad_kernel(meta, x, *refs, first):
    if first:
        acc, inner, (away, kept_o, low, term) = refs[0], refs[1:-4], refs[-4:]
        for k, part in enumerate(inner):
            rows = slice(k * CHUNK, (k + 1) * CHUNK)
            low[rows, :] = (acc[rows, :] + part[...]).astype(bf16)
    else:
        low, away, kept_o, term = refs
    number, half, rows, _ = away.shape
    w = term.shape[0]
    mine = lax.rem(meta[0], 2)
    for j in range(number):
        at = j if first else j + number
        term[...] = dot(x[:, at * w : (at + 1) * w], low[...], 0, 0)
        for i in range(half):
            kept_o[j, i] = term[span(2 * i + mine, rows), :].astype(bf16)
            away[j, i] = term[span(2 * i + 1 - mine, rows), :].astype(bf16)


def weight_grad(meta, x, sources, first):
    t, d = x.shape
    n2 = sources[0].shape[1]
    along, count = lax.axis_size("seq"), lax.axis_size("fsdp")
    w = d // along
    number = along // 2
    blocks = (number, count // 2, w // count, n2)
    out_shape = [shape(blocks, bf16), kept(blocks, bf16)] + ([kept((t, n2), bf16)] if first else [])
    return pl.pallas_call(
        functools.partial(weight_grad_kernel, first=first),
        in_specs=[SM, VM] + [VM] * len(sources),
        out_specs=[VM] * len(out_shape),
        out_shape=out_shape,
        scratch_shapes=[pltpu.VMEM((w, n2), f32)],
        compiler_params=params(8),
        cost_estimate=cost(2 * t * w * number * n2, 2 * t * w * number),
    )(meta, near(x), *map(near, sources))


def piece_kernel(x, v, g, cot, newest, p, sl, dl, si, di, half, skip, a, b, *refs, piece, at, ps):
    rebuilt_o, back_o, rhs, lhs = refs[-4:]
    q, w = rebuilt_o.shape
    n = p.shape[1] // 2
    per = w // ps
    k = pl.program_id(0)
    rows = span(k, q)
    cols = slice(piece * w, (piece + 1) * w)
    here = slice(at * w, (at + 1) * w)
    ahead = jnp.ones((1, w), f32)
    behind = ahead
    for j in range(half.shape[0]):
        hj = half[j, 0:1, cols]
        sq = hj * hj
        own = jnp.where(j == k, hj, 1.0)
        ahead = ahead * jnp.where(j < k, sq, own)
        behind = behind * jnp.where(j > k, sq, own)
    entry, readout = p[rows, :n], p[rows, n:]
    scores = jnp.where(causal(q), dot(readout, entry, 1, 1), 0.0)
    lhs[:, :q] = scores.astype(bf16)
    lhs[:, q:] = readout
    rhs[:q, :] = v[rows, cols]
    rhs[q:, :] = (sl[k, :, here].astype(f32) + si[piece].astype(f32) * ahead).astype(bf16)
    mixed = dot(lhs[...], rhs[...], 1, 0)
    av, bv = a[rows, :], b[rows, :]
    for h in range(per):
        hh = piece * per + h
        own = slice(h * ps, (h + 1) * ps)
        wide = slice(hh * ps, (hh + 1) * ps)
        y = mixed[:, own] * av[:, hh : hh + 1] + skip[0:1, wide] * x[rows, wide].astype(f32)
        rebuilt_o[:, own] = (newest[rows, wide].astype(f32) - y).astype(bf16)
    lhs[:, :q] = scores.T.astype(bf16)
    lhs[:, q:] = entry
    rhs[:q, :] = g[rows, cols]
    rhs[q:, :] = (dl[k, :, here].astype(f32) + di[piece].astype(f32) * behind).astype(bf16)
    back = dot(lhs[...], rhs[...], 1, 0)
    for h in range(per):
        hh = piece * per + h
        own = slice(h * ps, (h + 1) * ps)
        wide = slice(hh * ps, (hh + 1) * ps)
        gr = back[:, own] * bv[:, hh : hh + 1] + skip[0:1, wide] * cot[rows, wide].astype(f32)
        back_o[rows, own] = gr.astype(bf16)


def state_piece(x, v, g, cot, newest, p, sl, dl, si, di, half, skip, a, b, piece, previous):
    t, d = x.shape
    n2 = p.shape[1]
    n = n2 // 2
    heads = a.shape[1]
    w = d // PIECES
    cols = pl.BlockSpec((CHUNK, w), lambda i: (i, piece))
    args = [near(x), near(v), near(g), near(cot), near(newest),
            *map(near, (p, sl, dl, si, di, half)), skip, near(a), near(b)]
    in_specs = [VM] * 14
    aliases = {}
    if previous is not None:
        aliases = {len(args): 0}
        args.append(previous)
        in_specs.append(pl.BlockSpec(memory_space=pltpu.HBM))
    return pl.pallas_call(
        functools.partial(piece_kernel, piece=piece, at=max(piece - 1, 0), ps=d // heads),
        grid=(t // CHUNK,),
        in_specs=in_specs,
        out_specs=[cols, VM],
        out_shape=[pltpu.HBM((t, d), bf16), kept((t, w), bf16)],
        scratch_shapes=[pltpu.VMEM((CHUNK + n, w), bf16), pltpu.VMEM((CHUNK, CHUNK + n), bf16)],
        input_output_aliases=aliases,
        compiler_params=params(8),
        cost_estimate=cost(8 * t * w * n, 18 * t * w),
    )(*args)


def finish_kernel(x, midcot, low, rstd, weights, *refs, first):
    backs = refs[:PIECES]
    grad_o, grad = refs[-2:]
    q, d = grad_o.shape
    rows = span(first + pl.program_id(0), q)
    lhs = low[rows, :]
    w = d // PIECES
    step = 256
    sums = jnp.zeros((q, 128), f32)
    for i in range(d // step):
        cols = slice(i * step, (i + 1) * step)
        inside = slice(i * step % w, i * step % w + step)
        gr = dot(lhs, weights[cols, :], 1, 1) + backs[i * step // w][rows, inside].astype(f32)
        grad[:, cols] = gr
        prod = gr * x[rows, cols].astype(f32)
        for c in range(step // 128):
            sums = sums + prod[:, c * 128 : (c + 1) * 128]
    scale = jnp.broadcast_to(rstd[rows, :], (q, 128))
    dots = jnp.broadcast_to(jnp.sum(sums, axis=-1, keepdims=True), (q, 128)) * (scale * (1.0 / d))
    for i in range(d // 128):
        cols = slice(i * 128, (i + 1) * 128)
        dx = scale * grad[:, cols] - x[rows, cols].astype(f32) * dots
        grad_o[:, cols] = (midcot[rows, cols].astype(f32) + dx).astype(bf16)


def finish(x, backs, midcot, low, rstd, weights, first, number, previous):
    t, d = x.shape
    n2 = low.shape[1]
    row = pl.BlockSpec((CHUNK, d), lambda i: (first + i, 0))
    args = [near(x), near(midcot), near(low), near(rstd), near(weights), *map(near, backs)]
    in_specs = [VM] * (5 + PIECES)
    aliases = {}
    if previous is not None:
        aliases = {len(args): 0}
        args.append(previous)
        in_specs.append(pl.BlockSpec(memory_space=pltpu.HBM))
    return pl.pallas_call(
        functools.partial(finish_kernel, first=first),
        grid=(number,),
        in_specs=in_specs,
        out_specs=row,
        out_shape=pltpu.HBM((t, d), bf16),
        scratch_shapes=[pltpu.VMEM((CHUNK, d), f32)],
        input_output_aliases=aliases,
        compiler_params=params(12),
        cost_estimate=cost(2 * number * CHUNK * d * n2, 8 * number * CHUNK * d),
    )(*args)


def flip(x, bit):
    count = lax.axis_size("fsdp")
    return lax.ppermute(x, "fsdp", [(i, i ^ bit) for i in range(count)])


def gather_weights(w):
    count = lax.axis_size("fsdp")
    rows = w.shape[0]
    if count == 8:
        across, along = flip(w, 2), flip(w, 4)
        mid = rows // 2
        held = [(0, 0, w), (2, 0, across), (4, 0, along),
                (6, 0, flip(across[:mid], 4)), (6, mid, flip(along[mid:], 2))]
        held += [(k | 1, lo, flip(a, 1)) for k, lo, a in held]
    else:
        held = [(0, 0, w)]
        bit = count // 2
        while bit:
            held += [(k | bit, lo, flip(a, bit)) for k, lo, a in held]
            bit //= 2
    return [(k, lo) for k, lo, _ in held], [a for _, _, a in held]


def halve(value, away, kept_o, mine, pos):
    low = 1 << pos
    for i in range(away.shape[1]):
        base = (i // low) * 2 * low + i % low
        kept_o[:, i] = value(base + mine * low)
        away[:, i] = value(base + (1 - mine) * low)


def fold_kernel(meta, *refs, first, left, right):
    f = meta[0]
    bit = lambda b: lax.rem(lax.div(f, b), 2)
    pos = lambda b, order: sorted(order).index(b)
    if first:
        k0, g0, k1, g1, al, kl, ar, kr, total = refs
        part = k0.shape[0]
        total[:part] = (k0[...].astype(f32) + g0[...].astype(f32)).astype(bf16)
        total[part:] = (k1[...].astype(f32) + g1[...].astype(f32)).astype(bf16)
        n = al.shape[-1]
        halve(lambda m: total[:, m, :, :n], al, kl, bit(left[0]), pos(left[0], left))
        halve(lambda m: total[:, m, :, n:], ar, kr, bit(right[0]), pos(right[0], right))
        return
    kl, gl, kr, gr, al_o, kl_o, ar_o, kr_o, tl, tr = refs
    tl[...] = (kl[...].astype(f32) + gl[...].astype(f32)).astype(bf16)
    tr[...] = (kr[...].astype(f32) + gr[...].astype(f32)).astype(bf16)
    halve(lambda m: tl[:, m], al_o, kl_o, bit(left[0]), pos(left[0], left))
    halve(lambda m: tr[:, m], ar_o, kr_o, bit(right[0]), pos(right[0], right))


def fold(meta, arrays, left, right, first):
    along, blocks, rows, n = arrays[0].shape
    if first:
        along, n = 2 * along, n // 2
    out = (along, blocks // 2, rows, n)
    vmem = pl.BlockSpec(memory_space=pltpu.VMEM)
    scratch = [pltpu.VMEM((along, blocks, rows, 2 * n), bf16)] if first else [pltpu.VMEM(arrays[0].shape, bf16)] * 2
    return pl.pallas_call(
        functools.partial(fold_kernel, first=first, left=left, right=right),
        in_specs=[pl.BlockSpec(memory_space=pltpu.SMEM)] + [vmem] * len(arrays),
        out_specs=[vmem] * 4,
        out_shape=[shape(out, bf16), kept(out, bf16)] * 2,
        scratch_shapes=scratch,
        compiler_params=params(10),
        cost_estimate=cost(0, 8 * along * blocks * rows * n),
    )(meta, *arrays)


def deal_kernel(meta, kl, gl, kr, gr, own, *refs):
    _, _, _, n = kl.shape
    sends, both = refs[:-1], refs[-1]
    z = meta[1]
    both[:, :, :n] = (kl[:, 0].astype(f32) + gl[:, 0].astype(f32)).astype(bf16)
    both[:, :, n:] = (kr[:, 0].astype(f32) + gr[:, 0].astype(f32)).astype(bf16)
    own[...] = both[z]
    for k, out in enumerate(sends, 1):
        out[...] = both[jnp.bitwise_xor(z, k)]


def deal(meta, arrays):
    along, _, rows, n = arrays[0].shape
    vmem = pl.BlockSpec(memory_space=pltpu.VMEM)
    return pl.pallas_call(
        deal_kernel,
        in_specs=[pl.BlockSpec(memory_space=pltpu.SMEM)] + [vmem] * 4,
        out_specs=[vmem] * along,
        out_shape=[shape((rows, 2 * n), bf16)] * along,
        scratch_shapes=[pltpu.VMEM((along, rows, 2 * n), bf16)],
        compiler_params=params(8),
        cost_estimate=cost(0, 8 * along * rows * n),
        name="deal",
    )(meta, *arrays)


def scatter_sum(meta, halves):
    along = lax.axis_size("seq")
    count = lax.axis_size("fsdp")
    left = [1 << i for i in range(1, count.bit_length() - 1)]
    right = left[::-1]
    arrays = []
    for away, stays in halves:
        arrays += [stays, flip(away, 1)]
    al, kl, ar, kr = fold(meta, arrays, left, right, True)
    for _ in range(len(left)):
        gl, gr = flip(al, left[0]), flip(ar, right[0])
        left, right = left[1:], right[1:]
        if left:
            al, kl, ar, kr = fold(meta, [kl, gl, kr, gr], left, right, False)
    own, *sends = deal(meta, [kl, gl, kr, gr])
    total = own.astype(f32)
    for k, block in enumerate(sends, 1):
        other = lax.ppermute(block, "seq", [(i, i ^ k) for i in range(along)])
        total = total + other.astype(f32)
    return total


def step(middle_state, newest_state, middle_cotangent, newest_cotangent, log_decay, state_weights, skip_gain):
    t, d = middle_state.shape[1:]
    heads = log_decay.shape[2]
    middle, newest, midcot, cot = middle_state[0], newest_state[0], middle_cotangent[0], newest_cotangent[0]
    meta = places()
    block = state_weights.shape[0]
    count = t // CHUNK
    keys, pieces = gather_weights(state_weights)
    x, rstd, a, b, half = normalize(meta, middle, log_decay[0])
    v, g = scale_heads(x, cot, a, b)
    p, weights = project(meta, x, keys, pieces, block)
    s0, d0, loc, dtot, sa, sb = states(meta, p, v, g, half, None)
    s1, d1, loc, dtot = states(meta, p, v, g, half, (loc, dtot))
    inner = [inner_grad(p, v, g, s0, d0, s1, d1, k) for k in range(count)]
    acc, heads_done = pass_states(meta, sa, sb, loc, dtot, v, g, half)
    *half0, low = weight_grad(meta, x, [acc, *inner], True)
    half1 = weight_grad(meta, x, [low], False)
    skip = jnp.repeat(skip_gain, d // heads)[None]
    rebuilt, backs = None, []
    for i in range(PIECES):
        sp, dp = heads_done[i]
        rebuilt, back = state_piece(
            x, v, g, cot, newest, p, s1 if i else s0, d1 if i else d0, sp, dp, half, skip, a, b, i, rebuilt)
        backs.append(back)
    gradient = None
    for i in range(2):
        gradient = finish(x, backs, midcot, low, rstd, weights,
                          i * count // 2, count // 2, gradient)
    summed = scatter_sum(meta, [half0, half1])
    scale = (t * lax.axis_size("seq") * lax.axis_size("fsdp")) ** (-0.5)
    return rebuilt[None], gradient[None], summed * scale


def solution(mesh):
    whole = P("fsdp", "seq", None)
    return jax.shard_map(
        step,
        mesh=mesh,
        in_specs=(whole, whole, whole, whole, whole, P("fsdp", None), P()),
        out_specs=(whole, whole, P(("seq", "fsdp"), None)),
        check_vma=False,
    )
```

```python
import functools

import jax
import jax.numpy as jnp
from jax import lax
from jax.experimental import pallas as pl
from jax.experimental.pallas import tpu as pltpu
from jax.sharding import PartitionSpec as P


CHUNK = 128
PIECES = 4
MIB = 1024 * 1024

f32 = jnp.float32
bf16 = jnp.bfloat16
norm_epsilon = 1e-05
decay_unit = 1.0 / 4096.0


def dot(a, b, ca, cb):
    return lax.dot_general(a, b, (((ca,), (cb,)), ((), ())), preferred_element_type=f32)


def params(mib):
    return pltpu.CompilerParams(vmem_limit_bytes=mib * MIB)


def cost(flops, nbytes):
    return pl.CostEstimate(flops=int(flops), bytes_accessed=int(nbytes), transcendentals=0)


def shape(s, d):
    return jax.ShapeDtypeStruct(s, d)


def near(x):
    return pltpu.with_memory_space_constraint(x, pltpu.VMEM)


def kept(s, d):
    return pltpu.VMEM(s, d)


def span(i, n):
    return pl.ds(pl.multiple_of(i * n, n), n)


VM = pl.BlockSpec(memory_space=pltpu.VMEM)
SM = pl.BlockSpec(memory_space=pltpu.SMEM)


def normalize_kernel(meta, mid, decay, x_o, rstd_o, a_o, b_o, half_o, *, heads):
    del meta
    q, d = CHUNK, mid.shape[1]
    ps = d // heads
    own = span(pl.program_id(0), q)
    values = mid[own, :].astype(f32)
    rstd = lax.rsqrt(jnp.mean(values * values, axis=-1, keepdims=True) + norm_epsilon)
    i = pl.program_id(0)
    rstd_o[own, :] = rstd
    x_o[own, :] = (values * rstd).astype(bf16)
    rates = decay[...].astype(f32)
    running = (
        jnp.dot(causal(q).astype(f32), rates, precision=lax.Precision.HIGHEST, preferred_element_type=f32)
        * decay_unit
    )
    mid_log = 0.5 * running[q - 1 : q, :]
    a_o[own, :] = jnp.exp(running - mid_log) * (ps ** (-0.5))
    b_o[own, :] = jnp.exp(mid_log - running) * jnp.sqrt(1.0 - jnp.exp(2.0 * (rates * decay_unit)))
    half = jnp.exp(mid_log)
    for h in range(heads):
        half_o[i, :, h * ps : (h + 1) * ps] = jnp.broadcast_to(half[:, h : h + 1], (8, ps))


def normalize(meta, mid, decay):
    t, d = mid.shape
    heads = decay.shape[1]
    n = t // CHUNK
    row = lambda w: pl.BlockSpec((CHUNK, w), lambda i: (i, 0))
    return pl.pallas_call(
        functools.partial(normalize_kernel, heads=heads),
        grid=(n,),
        in_specs=[SM, VM, row(heads)],
        out_specs=[VM] * 5,
        out_shape=[kept((t, d), bf16), kept((t, 1), f32), kept((t, heads), f32), kept((t, heads), f32),
                   kept((n, 8, d), f32)],
        compiler_params=params(12),
        cost_estimate=cost(30 * t * d, 4 * t * d),
        name="normalize",
    )(meta, near(mid), decay)


def scale_heads_kernel(x, cot, a, b, v_o, g_o, spread):
    q, d = CHUNK, cot.shape[1]
    heads = a.shape[1]
    ps = d // heads
    i = pl.program_id(0)

    @pl.when(i == 0)
    def _():
        head = lax.rem(lax.broadcasted_iota(jnp.int32, spread.shape, 0), heads)
        col = lax.div(lax.broadcasted_iota(jnp.int32, spread.shape, 1), ps)
        spread[...] = jnp.where(head == col, 1.0, 0.0).astype(bf16)

    own = span(i, q)
    both = jnp.concatenate([a[own, :], b[own, :]], axis=0)
    high = both.astype(bf16)
    low = (both - high.astype(f32)).astype(bf16)
    parts = jnp.concatenate([high, low], axis=1)
    w = 4 * ps
    for c in range(d // w):
        cols = slice(c * w, (c + 1) * w)
        wide = dot(parts, spread[:, cols], 1, 0)
        v_o[own, cols] = (x[own, cols].astype(f32) * wide[q:]).astype(bf16)
        g_o[own, cols] = (cot[own, cols].astype(f32) * wide[:q]).astype(bf16)


def scale_heads(x, cot, a, b):
    t, d = x.shape
    return pl.pallas_call(
        scale_heads_kernel,
        grid=(t // CHUNK,),
        in_specs=[VM] * 4,
        out_specs=[VM, VM],
        out_shape=[kept((t, d), bf16)] * 2,
        scratch_shapes=[pltpu.VMEM((2 * a.shape[1], d), bf16)],
        compiler_params=params(8),
        cost_estimate=cost(10 * t * d, 8 * t * d),
        name="scale_heads",
    )(near(x), near(cot), near(a), near(b))


def project_kernel(meta, x, *refs, keys, block):
    weights, (out, full) = refs[:-2], refs[-2:]
    f = meta[0]
    total = None
    for (k, lo), w in zip(keys, weights):
        start = pl.multiple_of(jnp.bitwise_xor(f, k) * block + lo, 128)
        full[pl.ds(start, w.shape[0]), :] = w[...]
        part = dot(x[:, pl.ds(start, w.shape[0])], w[...], 1, 0)
        total = part if total is None else total + part
    out[...] = total.astype(bf16)


def project(meta, x, keys, pieces, block):
    t, d = x.shape
    n2 = pieces[0].shape[1]
    full = pl.BlockSpec(memory_space=pltpu.VMEM)
    return pl.pallas_call(
        functools.partial(project_kernel, keys=keys, block=block),
        in_specs=[pl.BlockSpec(memory_space=pltpu.SMEM), full] + [full] * len(pieces),
        out_specs=[full, full],
        out_shape=[kept((t, n2), bf16), kept((d, n2), bf16)],
        compiler_params=params(16),
        cost_estimate=cost(2 * t * d * n2, 2 * (t * d + d * n2)),
        name="project",
    )(meta, near(x), *pieces)


def states_kernel(meta, p, v, g, half, *refs, first, pieces):
    sl_o, dl_o, loc_o, dtot_o = refs[:4] if first else refs[-4:]
    t, d = v.shape
    w = d // PIECES
    n = p.shape[1] // 2
    count = t // CHUNK
    for at, piece in enumerate(pieces):
        cols = slice(piece * w, (piece + 1) * w)
        here = slice(at * w, (at + 1) * w)
        state = jnp.zeros((n, w), f32)
        total = jnp.ones((8, w), f32)
        for k in range(count):
            rows = slice(k * CHUNK, (k + 1) * CHUNK)
            hk = half[k, 0:1, cols]
            state = state * hk
            sl_o[k, :, here] = state.astype(bf16)
            state = (state + dot(p[rows, :n], v[rows, cols], 0, 0)) * hk
            total = total * half[k, :, cols] * half[k, :, cols]
        onward = state
        loc_o[0, piece] = onward.astype(bf16)
        dtot_o[:, cols] = total
        state = jnp.zeros((n, w), f32)
        for k in reversed(range(count)):
            rows = slice(k * CHUNK, (k + 1) * CHUNK)
            hk = half[k, 0:1, cols]
            state = state * hk
            dl_o[k, :, here] = state.astype(bf16)
            state = (state + dot(p[rows, n:], g[rows, cols], 0, 0)) * hk
        loc_o[1, piece] = state.astype(bf16)
        if first:
            oa, ob = refs[4:]
            odd = meta[2] == 1
            oa[...] = jnp.where(odd, state, onward).astype(bf16)
            ob[...] = jnp.where(odd, onward, state).astype(bf16)


def states(meta, p, v, g, half, previous):
    t, d = v.shape
    n = p.shape[1] // 2
    count = t // CHUNK
    w = d // PIECES
    first = previous is None
    pieces = range(1) if first else range(1, PIECES)
    number = len(pieces)
    args = [meta, near(p), near(v), near(g), near(half)]
    out_shape = [kept((count, n, number * w), bf16)] * 2 + [kept((2, PIECES, n, w), bf16), kept((8, d), f32)]
    aliases = {}
    if first:
        out_shape += [shape((n, w), bf16)] * 2
    else:
        aliases = {5: 2, 6: 3}
        args += [near(previous[0]), near(previous[1])]
    return pl.pallas_call(
        functools.partial(states_kernel, first=first, pieces=pieces),
        in_specs=[SM] + [VM] * (len(args) - 1),
        out_specs=[VM] * len(out_shape),
        out_shape=out_shape,
        input_output_aliases=aliases,
        compiler_params=params(8),
        cost_estimate=cost(4 * t * w * n * number, 8 * t * w * number),
    )(*args)


def turn_kernel(meta, x, away, kept_o, held, *, rows):
    g = held.shape[0]
    mine = lax.rem(meta[0], 2)
    for i in range(x.shape[1] // g):
        held[...] = x[:, i * g : (i + 1) * g].T
        for b in range(g // (2 * rows)):
            at = i * g // (2 * rows) + b
            kept_o[at * rows : (at + 1) * rows, :] = held[span(2 * b + mine, rows), :]
            away[at * rows : (at + 1) * rows, :] = held[span(2 * b + 1 - mine, rows), :]


def turn(meta, x):
    t, d = x.shape
    rows = d // (lax.axis_size("seq") * lax.axis_size("fsdp"))
    return pl.pallas_call(
        functools.partial(turn_kernel, rows=rows),
        in_specs=[SM, VM],
        out_specs=[VM, VM],
        out_shape=[shape((d // 2, t), bf16), kept((d // 2, t), bf16)],
        scratch_shapes=[pltpu.VMEM((4 * CHUNK, t), bf16)],
        compiler_params=params(6),
        cost_estimate=cost(0, 4 * t * d),
        name="turn",
    )(meta, near(x))


def hop_kernel(ids, ra, rb, loc, dtot, oa, ob, *, j):
    w = ra.shape[1]
    base = 2 + 8 * j
    for c, came, out in ((0, rb, oa), (2, ra, ob)):
        at = ids[base + c + 1]
        decay = dtot[0:1, span(at, w)]
        out[...] = (loc[ids[base + c], at].astype(f32) + decay * came[...].astype(f32)).astype(bf16)


def hop(ids, j, ra, rb, loc, dtot):
    n, w = ra.shape
    return pl.pallas_call(
        functools.partial(hop_kernel, j=j),
        in_specs=[SM] + [VM] * 4,
        out_specs=[VM, VM],
        out_shape=[shape((n, w), bf16)] * 2,
        compiler_params=params(4),
        cost_estimate=cost(4 * n * w, 12 * n * w),
    )(ids, ra, rb, near(loc), near(dtot))


def absorb_kernel(ids, ra, rb, v, g, half, *refs, j, fresh):
    si_o, di_o, acc = refs[-3:]
    t = v.shape[0]
    n, w = ra.shape
    count = t // CHUNK
    base = 2 + 8 * j
    odd = ids[base] == 1
    fa = ra[...].astype(f32)
    fb = rb[...].astype(f32)
    ahead = jnp.where(odd, fa, fb)
    behind = jnp.where(odd, fb, fa)
    if fresh:
        si_o[...] = jnp.zeros_like(si_o)
        di_o[...] = jnp.zeros_like(di_o)
        acc[...] = jnp.zeros_like(acc)
    si_o[ids[base + 5]] = ahead.astype(bf16)
    di_o[ids[base + 7]] = behind.astype(bf16)
    for c, state, order, other, part in ((4, ahead, range(count), g, slice(n, 2 * n)),
                                         (6, behind, reversed(range(count)), v, slice(0, n))):
        at = ids[base + c]

        @pl.when(at == ids[base + c + 1])
        def _():
            cols = span(at, w)
            carry = jnp.ones((1, w), f32)
            for k in order:
                rows = slice(k * CHUNK, (k + 1) * CHUNK)
                hk = half[k, 0:1, cols]
                acc[rows, part] += dot(other[rows, cols], (state * (carry * hk)).astype(bf16), 1, 1)
                carry = carry * hk * hk


def absorb(ids, j, ra, rb, v, g, half, held):
    t, _ = v.shape
    n, w = ra.shape
    args = [ids, ra, rb, near(v), near(g), near(half)]
    aliases = {}
    if held is not None:
        aliases = {6: 0, 7: 1, 8: 2}
        args += map(near, held)
    return pl.pallas_call(
        functools.partial(absorb_kernel, j=j, fresh=held is None),
        in_specs=[SM] + [VM] * (len(args) - 1),
        out_specs=[VM] * 3,
        out_shape=[kept((PIECES + 1, n, w), bf16)] * 2 + [kept((t, 2 * n), f32)],
        input_output_aliases=aliases,
        compiler_params=params(6),
        cost_estimate=cost(4 * t * w * n, 4 * t * w),
    )(*args)


def places():
    count = lax.axis_size("seq")
    z = lax.axis_index("seq")
    j = jnp.arange(PIECES + count - 2, dtype=jnp.int32)
    odd = jnp.zeros_like(j) + z % 2
    clip = lambda at: jnp.clip(at, 0, PIECES - 1)
    slot = lambda at: jnp.where((at >= 0) & (at < PIECES), at, PIECES)
    ahead, behind = j - z, j - (count - 1 - z)
    first = jnp.where(odd == 1, behind, ahead)
    second = jnp.where(odd == 1, ahead, behind)
    ids = jnp.stack(
        [odd, clip(first), 1 - odd, clip(second),
         clip(ahead + 1), slot(ahead + 1), clip(behind + 1), slot(behind + 1)], axis=1).reshape(-1)
    own = jnp.stack([lax.axis_index("fsdp"), z]).astype(jnp.int32)
    return jnp.concatenate([own, ids])


def pass_states(ids, sa, sb, loc, dtot, v, g, half):
    count = lax.axis_size("seq")
    steps = PIECES + count - 2
    pairs_a = [(i, i ^ 1) for i in range(count) if i ^ 1 < count]
    pairs_b = [p for i in range(1, count - 1, 2) for p in ((i, i + 1), (i + 1, i))]
    held = None
    done = []
    for step in range(steps):
        if step:
            sa, sb = hop(ids, step, ra, rb, loc, dtot)
        ra = lax.ppermute(sa, "seq", pairs_a)
        rb = lax.ppermute(sb, "seq", pairs_b)
        held = absorb(ids, step, ra, rb, v, g, half, held)
        if step >= count - 2:
            done.append(held[:2])
    return held[2], done


def causal(q):
    return lax.broadcasted_iota(jnp.int32, (q, q), 0) >= lax.broadcasted_iota(jnp.int32, (q, q), 1)


def inner_grad_kernel(p, v, g, sa, da, sb, db, out, *, k):
    n = p.shape[1] // 2
    w = sa.shape[2]
    rows = slice(k * CHUNK, (k + 1) * CHUNK)
    entry, readout = p[rows, :n], p[rows, n:]
    scores = jnp.where(causal(CHUNK), dot(g[rows, :], v[rows, :], 1, 1), 0.0).astype(bf16)
    out[:, :n] = dot(scores, readout, 0, 0) + dot(v[rows, :w], da[k], 1, 1) + dot(v[rows, w:], db[k], 1, 1)
    out[:, n:] = dot(scores, entry, 1, 0) + dot(g[rows, :w], sa[k], 1, 1) + dot(g[rows, w:], sb[k], 1, 1)


def inner_grad(p, v, g, sa, da, sb, db, k):
    _, d = v.shape
    n2 = p.shape[1]
    return pl.pallas_call(
        functools.partial(inner_grad_kernel, k=k),
        in_specs=[VM] * 7,
        out_specs=VM,
        out_shape=kept((CHUNK, n2), f32),
        compiler_params=params(6),
        cost_estimate=cost(6 * CHUNK * d * CHUNK, 8 * CHUNK * d),
    )(*map(near, (p, v, g, sa, da, sb, db)))


def lower_kernel(acc, *refs):
    inner, low = refs[:-1], refs[-1]
    for k, part in enumerate(inner):
        rows = slice(k * CHUNK, (k + 1) * CHUNK)
        low[rows, :] = (acc[rows, :] + part[...]).astype(bf16)


def lower(acc, inner):
    return pl.pallas_call(
        lower_kernel,
        in_specs=[VM] * (1 + len(inner)),
        out_specs=VM,
        out_shape=kept(acc.shape, bf16),
        compiler_params=params(4),
        cost_estimate=cost(0, 10 * acc.size),
        name="lower",
    )(near(acc), *map(near, inner))


def own_term_kernel(x, low, out):
    w = 4 * CHUNK
    for i in range(x.shape[0] // w):
        rows = slice(i * w, (i + 1) * w)
        out[rows, :] = dot(x[rows, :], low[...], 1, 0)


def own_term(x, low):
    d, t = x.shape
    n2 = low.shape[1]
    return pl.pallas_call(
        own_term_kernel,
        in_specs=[VM, VM],
        out_specs=VM,
        out_shape=kept((d, n2), f32),
        compiler_params=params(6),
        cost_estimate=cost(2 * t * d * n2, 2 * t * d),
        name="own_term",
    )(near(x), near(low))


def chip_term_kernel(meta, x, low, term, al, kl, ar, kr, total, *, left, right):
    along, blocks, rows, n2 = total.shape
    w = blocks * rows
    for s in range(along):
        own = slice(s * w, (s + 1) * w)
        value = (term[own, :] + dot(x[own, :], low[...], 1, 0)).astype(bf16)
        for i in range(blocks):
            total[s, i] = value[i * rows : (i + 1) * rows, :]
    n = n2 // 2
    f = meta[0]
    bit = lambda b: lax.rem(lax.div(f, b), 2)
    halve(lambda m: total[:, m, :, :n], al, kl, bit(left[0]), sorted(left).index(left[0]))
    halve(lambda m: total[:, m, :, n:], ar, kr, bit(right[0]), sorted(right).index(right[0]))


def chip_term(meta, x, low, term, left, right):
    d, t = x.shape
    n2 = low.shape[1]
    along, count = lax.axis_size("seq"), lax.axis_size("fsdp")
    blocks = count // 2
    rows = d // (along * blocks)
    out = (along, blocks // 2, rows, n2 // 2)
    return pl.pallas_call(
        functools.partial(chip_term_kernel, left=left, right=right),
        in_specs=[SM] + [VM] * 3,
        out_specs=[VM] * 4,
        out_shape=[shape(out, bf16), kept(out, bf16)] * 2,
        scratch_shapes=[pltpu.VMEM((along, blocks, rows, n2), bf16)],
        compiler_params=params(8),
        cost_estimate=cost(2 * t * d * n2, 2 * t * d),
        name="chip_term",
    )(meta, near(x), near(low), near(term))


def piece_kernel(x, v, g, cot, newest, p, sl, dl, si, di, half, skip, a, b, *refs, piece, at, ps):
    rebuilt_o, back_o, rhs, lhs = refs[-4:]
    q, w = rebuilt_o.shape
    n = p.shape[1] // 2
    per = w // ps
    k = pl.program_id(0)
    rows = span(k, q)
    cols = slice(piece * w, (piece + 1) * w)
    here = slice(at * w, (at + 1) * w)
    ahead = jnp.ones((1, w), f32)
    behind = ahead
    for j in range(half.shape[0]):
        hj = half[j, 0:1, cols]
        sq = hj * hj
        own = jnp.where(j == k, hj, 1.0)
        ahead = ahead * jnp.where(j < k, sq, own)
        behind = behind * jnp.where(j > k, sq, own)
    entry, readout = p[rows, :n], p[rows, n:]
    scores = jnp.where(causal(q), dot(readout, entry, 1, 1), 0.0)
    lhs[:, :q] = scores.astype(bf16)
    lhs[:, q:] = readout
    rhs[:q, :] = v[rows, cols]
    rhs[q:, :] = (sl[k, :, here].astype(f32) + si[piece].astype(f32) * ahead).astype(bf16)
    mixed = dot(lhs[...], rhs[...], 1, 0)
    av, bv = a[rows, :], b[rows, :]
    for h in range(per):
        hh = piece * per + h
        own = slice(h * ps, (h + 1) * ps)
        wide = slice(hh * ps, (hh + 1) * ps)
        y = mixed[:, own] * av[:, hh : hh + 1] + skip[0:1, wide] * x[rows, wide].astype(f32)
        rebuilt_o[:, own] = (newest[rows, wide].astype(f32) - y).astype(bf16)
    lhs[:, :q] = scores.T.astype(bf16)
    lhs[:, q:] = entry
    rhs[:q, :] = g[rows, cols]
    rhs[q:, :] = (dl[k, :, here].astype(f32) + di[piece].astype(f32) * behind).astype(bf16)
    back = dot(lhs[...], rhs[...], 1, 0)
    for h in range(per):
        hh = piece * per + h
        own = slice(h * ps, (h + 1) * ps)
        wide = slice(hh * ps, (hh + 1) * ps)
        gr = back[:, own] * bv[:, hh : hh + 1] + skip[0:1, wide] * cot[rows, wide].astype(f32)
        back_o[rows, own] = gr.astype(bf16)


def state_piece(x, v, g, cot, newest, p, sl, dl, si, di, half, skip, a, b, piece, previous):
    t, d = x.shape
    n2 = p.shape[1]
    n = n2 // 2
    heads = a.shape[1]
    w = d // PIECES
    cols = pl.BlockSpec((CHUNK, w), lambda i: (i, piece))
    args = [near(x), near(v), near(g), near(cot), near(newest),
            *map(near, (p, sl, dl, si, di, half)), skip, near(a), near(b)]
    in_specs = [VM] * 14
    aliases = {}
    if previous is not None:
        aliases = {len(args): 0}
        args.append(previous)
        in_specs.append(pl.BlockSpec(memory_space=pltpu.HBM))
    return pl.pallas_call(
        functools.partial(piece_kernel, piece=piece, at=max(piece - 1, 0), ps=d // heads),
        grid=(t // CHUNK,),
        in_specs=in_specs,
        out_specs=[cols, VM],
        out_shape=[pltpu.HBM((t, d), bf16), kept((t, w), bf16)],
        scratch_shapes=[pltpu.VMEM((CHUNK + n, w), bf16), pltpu.VMEM((CHUNK, CHUNK + n), bf16)],
        input_output_aliases=aliases,
        compiler_params=params(8),
        cost_estimate=cost(8 * t * w * n, 18 * t * w),
    )(*args)


def finish_kernel(x, midcot, low, rstd, weights, *refs, first):
    backs = refs[:PIECES]
    grad_o, grad = refs[-2:]
    q, d = grad_o.shape
    rows = span(first + pl.program_id(0), q)
    lhs = low[rows, :]
    w = d // PIECES
    step = 256
    sums = jnp.zeros((q, 128), f32)
    for i in range(d // step):
        cols = slice(i * step, (i + 1) * step)
        inside = slice(i * step % w, i * step % w + step)
        gr = dot(lhs, weights[cols, :], 1, 1) + backs[i * step // w][rows, inside].astype(f32)
        grad[:, cols] = gr
        prod = gr * x[rows, cols].astype(f32)
        for c in range(step // 128):
            sums = sums + prod[:, c * 128 : (c + 1) * 128]
    scale = jnp.broadcast_to(rstd[rows, :], (q, 128))
    dots = jnp.broadcast_to(jnp.sum(sums, axis=-1, keepdims=True), (q, 128)) * (scale * (1.0 / d))
    for i in range(d // 128):
        cols = slice(i * 128, (i + 1) * 128)
        dx = scale * grad[:, cols] - x[rows, cols].astype(f32) * dots
        grad_o[:, cols] = (midcot[rows, cols].astype(f32) + dx).astype(bf16)


def finish(x, backs, midcot, low, rstd, weights, first, number, previous):
    t, d = x.shape
    n2 = low.shape[1]
    row = pl.BlockSpec((CHUNK, d), lambda i: (first + i, 0))
    args = [near(x), near(midcot), near(low), near(rstd), near(weights), *map(near, backs)]
    in_specs = [VM] * (5 + PIECES)
    aliases = {}
    if previous is not None:
        aliases = {len(args): 0}
        args.append(previous)
        in_specs.append(pl.BlockSpec(memory_space=pltpu.HBM))
    return pl.pallas_call(
        functools.partial(finish_kernel, first=first),
        grid=(number,),
        in_specs=in_specs,
        out_specs=row,
        out_shape=pltpu.HBM((t, d), bf16),
        scratch_shapes=[pltpu.VMEM((CHUNK, d), f32)],
        input_output_aliases=aliases,
        compiler_params=params(12),
        cost_estimate=cost(2 * number * CHUNK * d * n2, 8 * number * CHUNK * d),
    )(*args)


def flip(x, bit):
    count = lax.axis_size("fsdp")
    return lax.ppermute(x, "fsdp", [(i, i ^ bit) for i in range(count)])


def gather_weights(w):
    count = lax.axis_size("fsdp")
    rows = w.shape[0]
    if count == 8:
        across, along = flip(w, 2), flip(w, 4)
        mid = rows // 2
        held = [(0, 0, w), (2, 0, across), (4, 0, along),
                (6, 0, flip(across[:mid], 4)), (6, mid, flip(along[mid:], 2))]
        held += [(k | 1, lo, flip(a, 1)) for k, lo, a in held]
    else:
        held = [(0, 0, w)]
        bit = count // 2
        while bit:
            held += [(k | bit, lo, flip(a, bit)) for k, lo, a in held]
            bit //= 2
    return [(k, lo) for k, lo, _ in held], [a for _, _, a in held]


def halve(value, away, kept_o, mine, pos):
    low = 1 << pos
    for i in range(away.shape[1]):
        base = (i // low) * 2 * low + i % low
        kept_o[:, i] = value(base + mine * low)
        away[:, i] = value(base + (1 - mine) * low)


def fold_kernel(meta, kl, gl, kr, gr, al_o, kl_o, ar_o, kr_o, tl, tr, *, left, right):
    f = meta[0]
    bit = lambda b: lax.rem(lax.div(f, b), 2)
    tl[...] = (kl[...].astype(f32) + gl[...].astype(f32)).astype(bf16)
    tr[...] = (kr[...].astype(f32) + gr[...].astype(f32)).astype(bf16)
    halve(lambda m: tl[:, m], al_o, kl_o, bit(left[0]), sorted(left).index(left[0]))
    halve(lambda m: tr[:, m], ar_o, kr_o, bit(right[0]), sorted(right).index(right[0]))


def fold(meta, arrays, left, right):
    along, blocks, rows, n = arrays[0].shape
    out = (along, blocks // 2, rows, n)
    return pl.pallas_call(
        functools.partial(fold_kernel, left=left, right=right),
        in_specs=[SM] + [VM] * 4,
        out_specs=[VM] * 4,
        out_shape=[shape(out, bf16), kept(out, bf16)] * 2,
        scratch_shapes=[pltpu.VMEM(arrays[0].shape, bf16)] * 2,
        compiler_params=params(10),
        cost_estimate=cost(0, 8 * along * blocks * rows * n),
    )(meta, *arrays)


def deal_kernel(meta, kl, gl, kr, gr, own, *refs):
    _, _, _, n = kl.shape
    sends, both = refs[:-1], refs[-1]
    z = meta[1]
    both[:, :, :n] = (kl[:, 0].astype(f32) + gl[:, 0].astype(f32)).astype(bf16)
    both[:, :, n:] = (kr[:, 0].astype(f32) + gr[:, 0].astype(f32)).astype(bf16)
    own[...] = both[z]
    for k, out in enumerate(sends, 1):
        out[...] = both[jnp.bitwise_xor(z, k)]


def deal(meta, arrays):
    along, _, rows, n = arrays[0].shape
    vmem = pl.BlockSpec(memory_space=pltpu.VMEM)
    return pl.pallas_call(
        deal_kernel,
        in_specs=[pl.BlockSpec(memory_space=pltpu.SMEM)] + [vmem] * 4,
        out_specs=[vmem] * along,
        out_shape=[shape((rows, 2 * n), bf16)] * along,
        scratch_shapes=[pltpu.VMEM((along, rows, 2 * n), bf16)],
        compiler_params=params(8),
        cost_estimate=cost(0, 8 * along * rows * n),
        name="deal",
    )(meta, *arrays)


def scatter_sum(meta, own, other, low):
    along = lax.axis_size("seq")
    count = lax.axis_size("fsdp")
    left = [1 << i for i in range(1, count.bit_length() - 1)]
    right = left[::-1]
    low_other = flip(low, 1)
    term = own_term(own, low)
    al, kl, ar, kr = chip_term(meta, other, low_other, term, left, right)
    for _ in range(len(left)):
        gl, gr = flip(al, left[0]), flip(ar, right[0])
        left, right = left[1:], right[1:]
        if left:
            al, kl, ar, kr = fold(meta, [kl, gl, kr, gr], left, right)
    own, *sends = deal(meta, [kl, gl, kr, gr])
    total = own.astype(f32)
    for k, block in enumerate(sends, 1):
        other = lax.ppermute(block, "seq", [(i, i ^ k) for i in range(along)])
        total = total + other.astype(f32)
    return total


def step(middle_state, newest_state, middle_cotangent, newest_cotangent, log_decay, state_weights, skip_gain):
    t, d = middle_state.shape[1:]
    heads = log_decay.shape[2]
    middle, newest, midcot, cot = middle_state[0], newest_state[0], middle_cotangent[0], newest_cotangent[0]
    meta = places()
    block = state_weights.shape[0]
    count = t // CHUNK
    keys, pieces = gather_weights(state_weights)
    x, rstd, a, b, half = normalize(meta, middle, log_decay[0])
    v, g = scale_heads(x, cot, a, b)
    p, weights = project(meta, x, keys, pieces, block)
    s0, d0, loc, dtot, sa, sb = states(meta, p, v, g, half, None)
    s1, d1, loc, dtot = states(meta, p, v, g, half, (loc, dtot))
    away, own = turn(meta, x)
    other = flip(away, 1)
    inner = [inner_grad(p, v, g, s0, d0, s1, d1, k) for k in range(count)]
    acc, heads_done = pass_states(meta, sa, sb, loc, dtot, v, g, half)
    low = lower(acc, inner)
    skip = jnp.repeat(skip_gain, d // heads)[None]
    rebuilt, backs = None, []
    for i in range(PIECES):
        sp, dp = heads_done[i]
        rebuilt, back = state_piece(
            x, v, g, cot, newest, p, s1 if i else s0, d1 if i else d0, sp, dp, half, skip, a, b, i, rebuilt)
        backs.append(back)
    gradient = None
    cuts = [0, count // 4, count // 2, count]
    for first, last in zip(cuts, cuts[1:]):
        if last > first:
            gradient = finish(x, backs, midcot, low, rstd, weights, first, last - first,
                              gradient)
    summed = scatter_sum(meta, own, other, low)
    scale = (t * lax.axis_size("seq") * lax.axis_size("fsdp")) ** (-0.5)
    return rebuilt[None], gradient[None], summed * scale


def solution(mesh):
    whole = P("fsdp", "seq", None)
    return jax.shard_map(
        step,
        mesh=mesh,
        in_specs=(whole, whole, whole, whole, whole, P("fsdp", None), P()),
        out_specs=(whole, whole, P(("seq", "fsdp"), None)),
        check_vma=False,
    )
```

```python
import functools

import jax
import jax.numpy as jnp
from jax import lax
from jax.experimental import pallas as pl
from jax.experimental.pallas import tpu as pltpu
from jax.sharding import PartitionSpec as P


CHUNK = 128
PIECES = 4
MIB = 1024 * 1024

f32 = jnp.float32
bf16 = jnp.bfloat16
norm_epsilon = 1e-05
decay_unit = 1.0 / 4096.0


def dot(a, b, ca, cb):
    return lax.dot_general(a, b, (((ca,), (cb,)), ((), ())), preferred_element_type=f32)


def params(mib):
    return pltpu.CompilerParams(vmem_limit_bytes=mib * MIB)


def cost(flops, nbytes):
    return pl.CostEstimate(flops=int(flops), bytes_accessed=int(nbytes), transcendentals=0)


def shape(s, d):
    return jax.ShapeDtypeStruct(s, d)


def near(x):
    return pltpu.with_memory_space_constraint(x, pltpu.VMEM)


def kept(s, d):
    return pltpu.VMEM(s, d)


def span(i, n):
    return pl.ds(pl.multiple_of(i * n, n), n)


VM = pl.BlockSpec(memory_space=pltpu.VMEM)
SM = pl.BlockSpec(memory_space=pltpu.SMEM)


def normalize_kernel(meta, mid, decay, x_o, rstd_o, a_o, b_o, half_o, *, heads):
    del meta
    q, d = CHUNK, mid.shape[1]
    ps = d // heads
    own = span(pl.program_id(0), q)
    values = mid[own, :].astype(f32)
    rstd = lax.rsqrt(jnp.mean(values * values, axis=-1, keepdims=True) + norm_epsilon)
    i = pl.program_id(0)
    rstd_o[own, :] = rstd
    x_o[own, :] = (values * rstd).astype(bf16)
    rates = decay[...].astype(f32)
    running = (
        jnp.dot(causal(q).astype(f32), rates, precision=lax.Precision.HIGHEST, preferred_element_type=f32)
        * decay_unit
    )
    mid_log = 0.5 * running[q - 1 : q, :]
    a_o[own, :] = jnp.exp(running - mid_log) * (ps ** (-0.5))
    b_o[own, :] = jnp.exp(mid_log - running) * jnp.sqrt(1.0 - jnp.exp(2.0 * (rates * decay_unit)))
    half = jnp.exp(mid_log)
    for h in range(heads):
        half_o[i, :, h * ps : (h + 1) * ps] = jnp.broadcast_to(half[:, h : h + 1], (8, ps))


def normalize(meta, mid, decay):
    t, d = mid.shape
    heads = decay.shape[1]
    n = t // CHUNK
    row = lambda w: pl.BlockSpec((CHUNK, w), lambda i: (i, 0))
    return pl.pallas_call(
        functools.partial(normalize_kernel, heads=heads),
        grid=(n,),
        in_specs=[SM, VM, row(heads)],
        out_specs=[VM] * 5,
        out_shape=[kept((t, d), bf16), kept((t, 1), f32), kept((t, heads), f32), kept((t, heads), f32),
                   kept((n, 8, d), f32)],
        compiler_params=params(12),
        cost_estimate=cost(30 * t * d, 4 * t * d),
        name="normalize",
    )(meta, near(mid), decay)


def scale_heads_kernel(x, cot, a, b, v_o, g_o, spread):
    q, d = CHUNK, cot.shape[1]
    heads = a.shape[1]
    ps = d // heads
    i = pl.program_id(0)

    @pl.when(i == 0)
    def _():
        head = lax.rem(lax.broadcasted_iota(jnp.int32, spread.shape, 0), heads)
        col = lax.div(lax.broadcasted_iota(jnp.int32, spread.shape, 1), ps)
        spread[...] = jnp.where(head == col, 1.0, 0.0).astype(bf16)

    own = span(i, q)
    both = jnp.concatenate([a[own, :], b[own, :]], axis=0)
    high = both.astype(bf16)
    low = (both - high.astype(f32)).astype(bf16)
    parts = jnp.concatenate([high, low], axis=1)
    w = 4 * ps
    for c in range(d // w):
        cols = slice(c * w, (c + 1) * w)
        wide = dot(parts, spread[:, cols], 1, 0)
        v_o[own, cols] = (x[own, cols].astype(f32) * wide[q:]).astype(bf16)
        g_o[own, cols] = (cot[own, cols].astype(f32) * wide[:q]).astype(bf16)


def scale_heads(x, cot, a, b):
    t, d = x.shape
    return pl.pallas_call(
        scale_heads_kernel,
        grid=(t // CHUNK,),
        in_specs=[VM] * 4,
        out_specs=[VM, VM],
        out_shape=[kept((t, d), bf16)] * 2,
        scratch_shapes=[pltpu.VMEM((2 * a.shape[1], d), bf16)],
        compiler_params=params(8),
        cost_estimate=cost(10 * t * d, 8 * t * d),
        name="scale_heads",
    )(near(x), near(cot), near(a), near(b))


def project_kernel(meta, x, *refs, keys, block):
    weights, (out, full) = refs[:-2], refs[-2:]
    f = meta[0]
    total = None
    for (k, lo), w in zip(keys, weights):
        start = pl.multiple_of(jnp.bitwise_xor(f, k) * block + lo, 128)
        full[pl.ds(start, w.shape[0]), :] = w[...]
        part = dot(x[:, pl.ds(start, w.shape[0])], w[...], 1, 0)
        total = part if total is None else total + part
    out[...] = total.astype(bf16)


def project(meta, x, keys, pieces, block):
    t, d = x.shape
    n2 = pieces[0].shape[1]
    full = pl.BlockSpec(memory_space=pltpu.VMEM)
    return pl.pallas_call(
        functools.partial(project_kernel, keys=keys, block=block),
        in_specs=[pl.BlockSpec(memory_space=pltpu.SMEM), full] + [full] * len(pieces),
        out_specs=[full, full],
        out_shape=[kept((t, n2), bf16), kept((d, n2), bf16)],
        compiler_params=params(16),
        cost_estimate=cost(2 * t * d * n2, 2 * (t * d + d * n2)),
        name="project",
    )(meta, near(x), *pieces)


def states_kernel(meta, p, v, g, half, *refs, first, pieces):
    sl_o, dl_o, loc_o, dtot_o = refs[:4] if first else refs[-4:]
    t, d = v.shape
    w = d // PIECES
    n = p.shape[1] // 2
    count = t // CHUNK
    for at, piece in enumerate(pieces):
        cols = slice(piece * w, (piece + 1) * w)
        here = slice(at * w, (at + 1) * w)
        state = jnp.zeros((n, w), f32)
        total = jnp.ones((8, w), f32)
        for k in range(count):
            rows = slice(k * CHUNK, (k + 1) * CHUNK)
            hk = half[k, 0:1, cols]
            state = state * hk
            sl_o[k, :, here] = state.astype(bf16)
            state = (state + dot(p[rows, :n], v[rows, cols], 0, 0)) * hk
            total = total * half[k, :, cols] * half[k, :, cols]
        onward = state
        loc_o[0, piece] = onward.astype(bf16)
        dtot_o[:, cols] = total
        state = jnp.zeros((n, w), f32)
        for k in reversed(range(count)):
            rows = slice(k * CHUNK, (k + 1) * CHUNK)
            hk = half[k, 0:1, cols]
            state = state * hk
            dl_o[k, :, here] = state.astype(bf16)
            state = (state + dot(p[rows, n:], g[rows, cols], 0, 0)) * hk
        loc_o[1, piece] = state.astype(bf16)
        if first:
            oa, ob = refs[4:]
            odd = meta[2] == 1
            oa[...] = jnp.where(odd, state, onward).astype(bf16)
            ob[...] = jnp.where(odd, onward, state).astype(bf16)


def states(meta, p, v, g, half, previous):
    t, d = v.shape
    n = p.shape[1] // 2
    count = t // CHUNK
    w = d // PIECES
    first = previous is None
    pieces = range(1) if first else range(1, PIECES)
    number = len(pieces)
    args = [meta, near(p), near(v), near(g), near(half)]
    out_shape = [kept((count, n, number * w), bf16)] * 2 + [kept((2, PIECES, n, w), bf16), kept((8, d), f32)]
    aliases = {}
    if first:
        out_shape += [shape((n, w), bf16)] * 2
    else:
        aliases = {5: 2, 6: 3}
        args += [near(previous[0]), near(previous[1])]
    return pl.pallas_call(
        functools.partial(states_kernel, first=first, pieces=pieces),
        in_specs=[SM] + [VM] * (len(args) - 1),
        out_specs=[VM] * len(out_shape),
        out_shape=out_shape,
        input_output_aliases=aliases,
        compiler_params=params(8),
        cost_estimate=cost(4 * t * w * n * number, 8 * t * w * number),
    )(*args)


def turn_kernel(meta, x, away, kept_o, held, *, rows):
    g = held.shape[0]
    mine = lax.rem(meta[0], 2)
    for i in range(x.shape[1] // g):
        held[...] = x[:, i * g : (i + 1) * g].T
        for b in range(g // (2 * rows)):
            at = i * g // (2 * rows) + b
            kept_o[at * rows : (at + 1) * rows, :] = held[span(2 * b + mine, rows), :]
            away[at * rows : (at + 1) * rows, :] = held[span(2 * b + 1 - mine, rows), :]


def turn(meta, x):
    t, d = x.shape
    rows = d // (lax.axis_size("seq") * lax.axis_size("fsdp"))
    return pl.pallas_call(
        functools.partial(turn_kernel, rows=rows),
        in_specs=[SM, VM],
        out_specs=[VM, VM],
        out_shape=[shape((d // 2, t), bf16), kept((d // 2, t), bf16)],
        scratch_shapes=[pltpu.VMEM((4 * CHUNK, t), bf16)],
        compiler_params=params(6),
        cost_estimate=cost(0, 4 * t * d),
        name="turn",
    )(meta, near(x))


def hop_kernel(ids, ra, rb, loc, dtot, oa, ob, *, j):
    w = ra.shape[1]
    base = 2 + 8 * j
    for c, came, out in ((0, rb, oa), (2, ra, ob)):
        at = ids[base + c + 1]
        decay = dtot[0:1, span(at, w)]
        out[...] = (loc[ids[base + c], at].astype(f32) + decay * came[...].astype(f32)).astype(bf16)


def hop(ids, j, ra, rb, loc, dtot):
    n, w = ra.shape
    return pl.pallas_call(
        functools.partial(hop_kernel, j=j),
        in_specs=[SM] + [VM] * 4,
        out_specs=[VM, VM],
        out_shape=[shape((n, w), bf16)] * 2,
        compiler_params=params(4),
        cost_estimate=cost(4 * n * w, 12 * n * w),
    )(ids, ra, rb, near(loc), near(dtot))


def absorb_kernel(ids, ra, rb, v, g, half, *refs, j, fresh):
    si_o, di_o, acc = refs[-3:]
    t = v.shape[0]
    n, w = ra.shape
    count = t // CHUNK
    base = 2 + 8 * j
    odd = ids[base] == 1
    fa = ra[...].astype(f32)
    fb = rb[...].astype(f32)
    ahead = jnp.where(odd, fa, fb)
    behind = jnp.where(odd, fb, fa)
    if fresh:
        si_o[...] = jnp.zeros_like(si_o)
        di_o[...] = jnp.zeros_like(di_o)
        acc[...] = jnp.zeros_like(acc)
    si_o[ids[base + 5]] = ahead.astype(bf16)
    di_o[ids[base + 7]] = behind.astype(bf16)
    for c, state, order, other, part in ((4, ahead, range(count), g, slice(n, 2 * n)),
                                         (6, behind, reversed(range(count)), v, slice(0, n))):
        at = ids[base + c]

        @pl.when(at == ids[base + c + 1])
        def _():
            cols = span(at, w)
            carry = jnp.ones((1, w), f32)
            for k in order:
                rows = slice(k * CHUNK, (k + 1) * CHUNK)
                hk = half[k, 0:1, cols]
                acc[rows, part] += dot(other[rows, cols], (state * (carry * hk)).astype(bf16), 1, 1)
                carry = carry * hk * hk


def absorb(ids, j, ra, rb, v, g, half, held):
    t, _ = v.shape
    n, w = ra.shape
    args = [ids, ra, rb, near(v), near(g), near(half)]
    aliases = {}
    if held is not None:
        aliases = {6: 0, 7: 1, 8: 2}
        args += map(near, held)
    return pl.pallas_call(
        functools.partial(absorb_kernel, j=j, fresh=held is None),
        in_specs=[SM] + [VM] * (len(args) - 1),
        out_specs=[VM] * 3,
        out_shape=[kept((PIECES + 1, n, w), bf16)] * 2 + [kept((t, 2 * n), f32)],
        input_output_aliases=aliases,
        compiler_params=params(6),
        cost_estimate=cost(4 * t * w * n, 4 * t * w),
    )(*args)


def places():
    count = lax.axis_size("seq")
    z = lax.axis_index("seq")
    j = jnp.arange(PIECES + count - 2, dtype=jnp.int32)
    odd = jnp.zeros_like(j) + z % 2
    clip = lambda at: jnp.clip(at, 0, PIECES - 1)
    slot = lambda at: jnp.where((at >= 0) & (at < PIECES), at, PIECES)
    ahead, behind = j - z, j - (count - 1 - z)
    first = jnp.where(odd == 1, behind, ahead)
    second = jnp.where(odd == 1, ahead, behind)
    ids = jnp.stack(
        [odd, clip(first), 1 - odd, clip(second),
         clip(ahead + 1), slot(ahead + 1), clip(behind + 1), slot(behind + 1)], axis=1).reshape(-1)
    own = jnp.stack([lax.axis_index("fsdp"), z]).astype(jnp.int32)
    return jnp.concatenate([own, ids])


def pass_states(ids, sa, sb, loc, dtot, v, g, half):
    count = lax.axis_size("seq")
    steps = PIECES + count - 2
    pairs_a = [(i, i ^ 1) for i in range(count) if i ^ 1 < count]
    pairs_b = [p for i in range(1, count - 1, 2) for p in ((i, i + 1), (i + 1, i))]
    held = None
    done = []
    for step in range(steps):
        if step:
            sa, sb = hop(ids, step, ra, rb, loc, dtot)
        ra = lax.ppermute(sa, "seq", pairs_a)
        rb = lax.ppermute(sb, "seq", pairs_b)
        held = absorb(ids, step, ra, rb, v, g, half, held)
        if step >= count - 2:
            done.append(held[:2])
    return held[2], done


def causal(q):
    return lax.broadcasted_iota(jnp.int32, (q, q), 0) >= lax.broadcasted_iota(jnp.int32, (q, q), 1)


def inner_grad_kernel(p, v, g, sa, da, sb, db, out, *, k):
    n = p.shape[1] // 2
    w = sa.shape[2]
    rows = slice(k * CHUNK, (k + 1) * CHUNK)
    entry, readout = p[rows, :n], p[rows, n:]
    scores = jnp.where(causal(CHUNK), dot(g[rows, :], v[rows, :], 1, 1), 0.0).astype(bf16)
    out[:, :n] = dot(scores, readout, 0, 0) + dot(v[rows, :w], da[k], 1, 1) + dot(v[rows, w:], db[k], 1, 1)
    out[:, n:] = dot(scores, entry, 1, 0) + dot(g[rows, :w], sa[k], 1, 1) + dot(g[rows, w:], sb[k], 1, 1)


def inner_grad(p, v, g, sa, da, sb, db, k):
    _, d = v.shape
    n2 = p.shape[1]
    return pl.pallas_call(
        functools.partial(inner_grad_kernel, k=k),
        in_specs=[VM] * 7,
        out_specs=VM,
        out_shape=kept((CHUNK, n2), f32),
        compiler_params=params(6),
        cost_estimate=cost(6 * CHUNK * d * CHUNK, 8 * CHUNK * d),
    )(*map(near, (p, v, g, sa, da, sb, db)))


def lower_kernel(acc, *refs):
    inner, low = refs[:-1], refs[-1]
    for k, part in enumerate(inner):
        rows = slice(k * CHUNK, (k + 1) * CHUNK)
        low[rows, :] = (acc[rows, :] + part[...]).astype(bf16)


def lower(acc, inner):
    return pl.pallas_call(
        lower_kernel,
        in_specs=[VM] * (1 + len(inner)),
        out_specs=VM,
        out_shape=kept(acc.shape, bf16),
        compiler_params=params(4),
        cost_estimate=cost(0, 10 * acc.size),
        name="lower",
    )(near(acc), *map(near, inner))


def own_term_kernel(x, low, out):
    w = 4 * CHUNK
    for i in range(x.shape[0] // w):
        rows = slice(i * w, (i + 1) * w)
        out[rows, :] = dot(x[rows, :], low[...], 1, 0)


def own_term(x, low):
    d, t = x.shape
    n2 = low.shape[1]
    return pl.pallas_call(
        own_term_kernel,
        in_specs=[VM, VM],
        out_specs=VM,
        out_shape=kept((d, n2), f32),
        compiler_params=params(6),
        cost_estimate=cost(2 * t * d * n2, 2 * t * d),
        name="own_term",
    )(near(x), near(low))


def chip_term_kernel(meta, x, low, term, al, kl, ar, kr, total, *, left, right):
    along, blocks, rows, n2 = total.shape
    w = blocks * rows
    for s in range(along):
        own = slice(s * w, (s + 1) * w)
        value = (term[own, :] + dot(x[own, :], low[...], 1, 0)).astype(bf16)
        for i in range(blocks):
            total[s, i] = value[i * rows : (i + 1) * rows, :]
    n = n2 // 2
    f = meta[0]
    bit = lambda b: lax.rem(lax.div(f, b), 2)
    halve(lambda m: total[:, m, :, :n], al, kl, bit(left[0]), sorted(left).index(left[0]))
    halve(lambda m: total[:, m, :, n:], ar, kr, bit(right[0]), sorted(right).index(right[0]))


def chip_term(meta, x, low, term, left, right):
    d, t = x.shape
    n2 = low.shape[1]
    along, count = lax.axis_size("seq"), lax.axis_size("fsdp")
    blocks = count // 2
    rows = d // (along * blocks)
    out = (along, blocks // 2, rows, n2 // 2)
    return pl.pallas_call(
        functools.partial(chip_term_kernel, left=left, right=right),
        in_specs=[SM] + [VM] * 3,
        out_specs=[VM] * 4,
        out_shape=[shape(out, bf16), kept(out, bf16)] * 2,
        scratch_shapes=[pltpu.VMEM((along, blocks, rows, n2), bf16)],
        compiler_params=params(8),
        cost_estimate=cost(2 * t * d * n2, 2 * t * d),
        name="chip_term",
    )(meta, near(x), near(low), near(term))


def piece_kernel(x, v, g, cot, newest, p, sl, dl, si, di, half, skip, a, b, *refs, piece, at, ps):
    rebuilt_o, back_o, dots_o, rhs, lhs = refs[-5:]
    q, w = rebuilt_o.shape
    n = p.shape[1] // 2
    per = w // ps
    k = pl.program_id(0)
    rows = span(k, q)
    cols = slice(piece * w, (piece + 1) * w)
    here = slice(at * w, (at + 1) * w)
    ahead = jnp.ones((1, w), f32)
    behind = ahead
    for j in range(half.shape[0]):
        hj = half[j, 0:1, cols]
        sq = hj * hj
        own = jnp.where(j == k, hj, 1.0)
        ahead = ahead * jnp.where(j < k, sq, own)
        behind = behind * jnp.where(j > k, sq, own)
    entry, readout = p[rows, :n], p[rows, n:]
    scores = jnp.where(causal(q), dot(readout, entry, 1, 1), 0.0)
    lhs[:, :q] = scores.astype(bf16)
    lhs[:, q:] = readout
    rhs[:q, :] = v[rows, cols]
    rhs[q:, :] = (sl[k, :, here].astype(f32) + si[piece].astype(f32) * ahead).astype(bf16)
    mixed = dot(lhs[...], rhs[...], 1, 0)
    av, bv = a[rows, :], b[rows, :]
    for h in range(per):
        hh = piece * per + h
        own = slice(h * ps, (h + 1) * ps)
        wide = slice(hh * ps, (hh + 1) * ps)
        y = mixed[:, own] * av[:, hh : hh + 1] + skip[0:1, wide] * x[rows, wide].astype(f32)
        rebuilt_o[:, own] = (newest[rows, wide].astype(f32) - y).astype(bf16)
    lhs[:, :q] = scores.T.astype(bf16)
    lhs[:, q:] = entry
    rhs[:q, :] = g[rows, cols]
    rhs[q:, :] = (dl[k, :, here].astype(f32) + di[piece].astype(f32) * behind).astype(bf16)
    back = dot(lhs[...], rhs[...], 1, 0)
    for h in range(per):
        hh = piece * per + h
        own = slice(h * ps, (h + 1) * ps)
        wide = slice(hh * ps, (hh + 1) * ps)
        gr = back[:, own] * bv[:, hh : hh + 1] + skip[0:1, wide] * cot[rows, wide].astype(f32)
        back_o[rows, own] = gr.astype(bf16)
        prod = gr * x[rows, wide].astype(f32)
        sums = prod if h == 0 else sums + prod
    dots_o[rows, :] = sums


def state_piece(x, v, g, cot, newest, p, sl, dl, si, di, half, skip, a, b, piece, previous):
    t, d = x.shape
    n2 = p.shape[1]
    n = n2 // 2
    heads = a.shape[1]
    w = d // PIECES
    cols = pl.BlockSpec((CHUNK, w), lambda i: (i, piece))
    args = [near(x), near(v), near(g), near(cot), near(newest),
            *map(near, (p, sl, dl, si, di, half)), skip, near(a), near(b)]
    in_specs = [VM] * 14
    aliases = {}
    if previous is not None:
        aliases = {len(args): 0}
        args.append(previous)
        in_specs.append(pl.BlockSpec(memory_space=pltpu.HBM))
    return pl.pallas_call(
        functools.partial(piece_kernel, piece=piece, at=max(piece - 1, 0), ps=d // heads),
        grid=(t // CHUNK,),
        in_specs=in_specs,
        out_specs=[cols, VM, VM],
        out_shape=[pltpu.HBM((t, d), bf16), kept((t, w), bf16), kept((t, d // heads), f32)],
        scratch_shapes=[pltpu.VMEM((CHUNK + n, w), bf16), pltpu.VMEM((CHUNK, CHUNK + n), bf16)],
        input_output_aliases=aliases,
        compiler_params=params(8),
        cost_estimate=cost(8 * t * w * n, 18 * t * w),
    )(*args)


def finish_kernel(x, midcot, low, p, rstd, weights, *refs, first):
    backs, sums = refs[:PIECES], refs[PIECES : 2 * PIECES]
    grad_o = refs[-1]
    q, d = CHUNK, x.shape[1]
    rows = span(first + pl.program_id(0), q)
    lhs = low[rows, :]
    w = d // PIECES
    step = 256
    both = lhs.astype(f32) * p[rows, :].astype(f32)
    total = sums[0][rows, :]
    for other in sums[1:]:
        total = total + other[rows, :]
    dots = jnp.sum(total, axis=-1, keepdims=True) + jnp.sum(both, axis=-1, keepdims=True)
    scale = jnp.broadcast_to(rstd[rows, :], (q, step))
    dots = jnp.broadcast_to(dots, (q, step)) * (scale * (1.0 / d))
    for i in range(d // step):
        cols = slice(i * step, (i + 1) * step)
        inside = slice(i * step % w, i * step % w + step)
        gr = dot(lhs, weights[cols, :], 1, 1) + backs[i * step // w][rows, inside].astype(f32)
        dx = scale * gr - x[rows, cols].astype(f32) * dots
        grad_o[:, cols] = (midcot[rows, cols].astype(f32) + dx).astype(bf16)


def finish(x, backs, sums, midcot, low, p, rstd, weights, first, number, previous):
    t, d = x.shape
    n2 = low.shape[1]
    row = pl.BlockSpec((CHUNK, d), lambda i: (first + i, 0))
    args = [*map(near, (x, midcot, low, p, rstd, weights)), *map(near, backs), *map(near, sums)]
    in_specs = [VM] * (6 + 2 * PIECES)
    aliases = {}
    if previous is not None:
        aliases = {len(args): 0}
        args.append(previous)
        in_specs.append(pl.BlockSpec(memory_space=pltpu.HBM))
    return pl.pallas_call(
        functools.partial(finish_kernel, first=first),
        grid=(number,),
        in_specs=in_specs,
        out_specs=row,
        out_shape=pltpu.HBM((t, d), bf16),
        input_output_aliases=aliases,
        compiler_params=params(8),
        cost_estimate=cost(2 * number * CHUNK * d * n2, 8 * number * CHUNK * d),
    )(*args)


def flip(x, bit):
    count = lax.axis_size("fsdp")
    return lax.ppermute(x, "fsdp", [(i, i ^ bit) for i in range(count)])


def gather_weights(w):
    count = lax.axis_size("fsdp")
    rows = w.shape[0]
    if count == 8:
        across, along = flip(w, 2), flip(w, 4)
        mid = rows // 2
        held = [(0, 0, w), (2, 0, across), (4, 0, along),
                (6, 0, flip(across[:mid], 4)), (6, mid, flip(along[mid:], 2))]
        held += [(k | 1, lo, flip(a, 1)) for k, lo, a in held]
    else:
        held = [(0, 0, w)]
        bit = count // 2
        while bit:
            held += [(k | bit, lo, flip(a, bit)) for k, lo, a in held]
            bit //= 2
    return [(k, lo) for k, lo, _ in held], [a for _, _, a in held]


def halve(value, away, kept_o, mine, pos):
    low = 1 << pos
    for i in range(away.shape[1]):
        base = (i // low) * 2 * low + i % low
        kept_o[:, i] = value(base + mine * low)
        away[:, i] = value(base + (1 - mine) * low)


def fold_kernel(meta, kl, gl, kr, gr, al_o, kl_o, ar_o, kr_o, tl, tr, *, left, right):
    f = meta[0]
    bit = lambda b: lax.rem(lax.div(f, b), 2)
    tl[...] = (kl[...].astype(f32) + gl[...].astype(f32)).astype(bf16)
    tr[...] = (kr[...].astype(f32) + gr[...].astype(f32)).astype(bf16)
    halve(lambda m: tl[:, m], al_o, kl_o, bit(left[0]), sorted(left).index(left[0]))
    halve(lambda m: tr[:, m], ar_o, kr_o, bit(right[0]), sorted(right).index(right[0]))


def fold(meta, arrays, left, right):
    along, blocks, rows, n = arrays[0].shape
    out = (along, blocks // 2, rows, n)
    return pl.pallas_call(
        functools.partial(fold_kernel, left=left, right=right),
        in_specs=[SM] + [VM] * 4,
        out_specs=[VM] * 4,
        out_shape=[shape(out, bf16), kept(out, bf16)] * 2,
        scratch_shapes=[pltpu.VMEM(arrays[0].shape, bf16)] * 2,
        compiler_params=params(10),
        cost_estimate=cost(0, 8 * along * blocks * rows * n),
    )(meta, *arrays)


def deal_kernel(meta, kl, gl, kr, gr, own, *refs):
    _, _, _, n = kl.shape
    sends, both = refs[:-1], refs[-1]
    z = meta[1]
    both[:, :, :n] = (kl[:, 0].astype(f32) + gl[:, 0].astype(f32)).astype(bf16)
    both[:, :, n:] = (kr[:, 0].astype(f32) + gr[:, 0].astype(f32)).astype(bf16)
    own[...] = both[z]
    for k, out in enumerate(sends, 1):
        out[...] = both[jnp.bitwise_xor(z, k)]


def deal(meta, arrays):
    along, _, rows, n = arrays[0].shape
    vmem = pl.BlockSpec(memory_space=pltpu.VMEM)
    return pl.pallas_call(
        deal_kernel,
        in_specs=[pl.BlockSpec(memory_space=pltpu.SMEM)] + [vmem] * 4,
        out_specs=[vmem] * along,
        out_shape=[shape((rows, 2 * n), bf16)] * along,
        scratch_shapes=[pltpu.VMEM((along, rows, 2 * n), bf16)],
        compiler_params=params(8),
        cost_estimate=cost(0, 8 * along * rows * n),
        name="deal",
    )(meta, *arrays)


def scatter_sum(meta, own, other, low):
    along = lax.axis_size("seq")
    count = lax.axis_size("fsdp")
    left = [1 << i for i in range(1, count.bit_length() - 1)]
    right = left[::-1]
    low_other = flip(low, 1)
    term = own_term(own, low)
    al, kl, ar, kr = chip_term(meta, other, low_other, term, left, right)
    for _ in range(len(left)):
        gl, gr = flip(al, left[0]), flip(ar, right[0])
        left, right = left[1:], right[1:]
        if left:
            al, kl, ar, kr = fold(meta, [kl, gl, kr, gr], left, right)
    own, *sends = deal(meta, [kl, gl, kr, gr])
    total = own.astype(f32)
    for k, block in enumerate(sends, 1):
        other = lax.ppermute(block, "seq", [(i, i ^ k) for i in range(along)])
        total = total + other.astype(f32)
    return total


def step(middle_state, newest_state, middle_cotangent, newest_cotangent, log_decay, state_weights, skip_gain):
    t, d = middle_state.shape[1:]
    heads = log_decay.shape[2]
    middle, newest, midcot, cot = middle_state[0], newest_state[0], middle_cotangent[0], newest_cotangent[0]
    meta = places()
    block = state_weights.shape[0]
    count = t // CHUNK
    keys, pieces = gather_weights(state_weights)
    x, rstd, a, b, half = normalize(meta, middle, log_decay[0])
    v, g = scale_heads(x, cot, a, b)
    p, weights = project(meta, x, keys, pieces, block)
    s0, d0, loc, dtot, sa, sb = states(meta, p, v, g, half, None)
    s1, d1, loc, dtot = states(meta, p, v, g, half, (loc, dtot))
    away, own = turn(meta, x)
    other = flip(away, 1)
    inner = [inner_grad(p, v, g, s0, d0, s1, d1, k) for k in range(count)]
    acc, heads_done = pass_states(meta, sa, sb, loc, dtot, v, g, half)
    low = lower(acc, inner)
    skip = jnp.repeat(skip_gain, d // heads)[None]
    rebuilt, backs, sums = None, [], []
    for i in range(PIECES):
        sp, dp = heads_done[i]
        rebuilt, back, dots = state_piece(
            x, v, g, cot, newest, p, s1 if i else s0, d1 if i else d0, sp, dp, half, skip, a, b, i, rebuilt)
        backs.append(back)
        sums.append(dots)
    gradient = None
    cuts = [0, count // 4, count // 2, count]
    for first, last in zip(cuts, cuts[1:]):
        if last > first:
            gradient = finish(x, backs, sums, midcot, low, p, rstd, weights, first, last - first,
                              gradient)
    summed = scatter_sum(meta, own, other, low)
    scale = (t * lax.axis_size("seq") * lax.axis_size("fsdp")) ** (-0.5)
    return rebuilt[None], gradient[None], summed * scale


def solution(mesh):
    whole = P("fsdp", "seq", None)
    return jax.shard_map(
        step,
        mesh=mesh,
        in_specs=(whole, whole, whole, whole, whole, P("fsdp", None), P()),
        out_specs=(whole, whole, P(("seq", "fsdp"), None)),
        check_vma=False,
    )
```
